128 devices in a mesh: seq: 32 (over x, y, core), tp: 4 (over z).
Axes of the slice: x: 4, y: 4, z: 4, core: 2. Of those that a mesh axis runs over, the one named last changes fastest.
Arguments:
- states_in: bfloat16 [8192, 2048], P('seq'), may hold values from -7 to 7
- lengths: int32 [4], replicated, may hold values from 1 to 64, 128 in all
- attn_gain: float32 [2048], replicated, may hold values from 0.5 to 1.5
- w_query: bfloat16 [2048, 2048], P(None, 'tp'), may hold values from -0.125 to 0.125
- w_key: bfloat16 [2048, 2048], P(None, 'tp'), may hold values from -0.088388348 to 0.088388348
- w_value: bfloat16 [2048, 4096], P(None, 'tp'), may hold values from -0.125 to 0.125
- w_gate: bfloat16 [2048, 4096], P(None, 'tp'), may hold values from -0.125 to 0.125
- w_beta: bfloat16 [2048, 16], P(None, 'tp'), may hold values from -1 to 1
- w_alpha: bfloat16 [2048, 16], P(None, 'tp'), may hold values from -0.125 to 0.125
- decay_rate: float32 [16], P('tp'), may hold values from 4.8828125e-05 to 0.05
- decay_bias: float32 [16], P('tp'), may hold values from -2 to 1
- conv_query: float32 [4, 2048], P(None, 'tp'), may hold values from -3 to 3
- conv_key: float32 [4, 2048], P(None, 'tp'), may hold values from -3 to 3
- conv_value: float32 [4, 4096], P(None, 'tp'), may hold values from -4.5 to 4.5
- out_gain: float32 [256], replicated, may hold values from 0.5 to 1.5
- w_out: bfloat16 [4096, 2048], P('tp'), may hold values from -0.09375 to 0.09375
- final_gain: float32 [2048], replicated, may hold values from 0.5 to 1.5
- w_head: bfloat16 [2048, 32000], P(None, ('seq', 'tp')), may hold values from -0.41992188 to 0.41992188
Outputs:
- hidden: bfloat16 [8192, 2048], P('seq', 'tp')
- block_states: float32 [128, 16, 128, 256], P('seq', 'tp')
- max_logit: float32 [4], replicated
The draws below stay inside these ranges and needn't reach their ends.
Inputs may be any that keep to these rules, and one draw needn't show every extreme that they name: Prompt lengths are counted in blocks of 64 tokens; they sum to 128 and the longest is 64.
All inputs are finite; a program needn't handle non-finite values.
Results may differ from the reference program's by a relative error of at most 0.0095.
Values may be sent and summed in bfloat16 or wider, within the bound.
No kernel may reach another device: no remote copies, remote signals or barrier semaphores. Data moves between devices by JAX's collectives and lax.ppermute only.
A program may use at most 128 MiB of HBM per device.

```python
import math
import jax
import jax.numpy as jnp
import numpy as np
from jax import lax

D = 2048
HEADS = 16
DK = 128
DV = 256
CONV = 4
BLOCK_LEN = 64
VOCAB = 32000
REQUESTS = 4
TOKENS = 8192
BLOCKS = 128
LONGEST = 64


level_height = 3.0


def feature_set(key):
    picked = jax.random.permutation(jax.random.fold_in(key, 101), D)
    return (picked < D // 16).astype(jnp.float32)


def common_row(key):
    chosen = feature_set(key)
    sign_values = 2.0 * jax.random.randint(jax.random.fold_in(key, 102), (D,), 0, 2).astype(jnp.float32) - 1.0
    return level_height * sign_values * chosen


def slow_heads(key, slow_count):
    picked = jax.random.permutation(jax.random.fold_in(key, 103), HEADS)
    return (picked < slow_count).astype(jnp.float32)


def slow_total():
    return HEADS // 2


def unit_draw(key, array_shape, clip_limit):
    return jnp.clip(jax.random.normal(key, array_shape, jnp.float32), -clip_limit, clip_limit)


def draw_states_in(key, part):
    random_part = unit_draw(jax.random.fold_in(key, 1), (TOKENS, D), 4.0)
    return (random_part + common_row(key)[None, :]).astype(jnp.bfloat16)


def draw_w_key(key, part):
    row_scale = 1.0 - 0.9 * feature_set(key)
    random_part = unit_draw(jax.random.fold_in(key, 2), (D, HEADS * DK), 4.0)
    return (random_part * D ** (-0.5) * row_scale[:, None]).astype(jnp.bfloat16)


def draw_w_beta(key, part):
    slow_mask = slow_heads(key, slow_total())
    strength = jnp.exp(jax.random.uniform(jax.random.fold_in(key, 3), (HEADS,), jnp.float32, math.log(0.3), math.log(0.8)))
    slow_shift = jnp.log(strength * (DK / (LONGEST * BLOCK_LEN)))
    fast_shift = jax.random.uniform(jax.random.fold_in(key, 4), (HEADS,), jnp.float32, -1.0, 1.0)
    beta_shift = slow_mask * slow_shift + (1.0 - slow_mask) * fast_shift
    level_scale = math.sqrt(1.0 + level_height * level_height / 16.0) / (D // 16 * level_height * level_height)
    random_part = unit_draw(jax.random.fold_in(key, 5), (D, HEADS), 4.0) * (0.5 * D ** (-0.5))
    return (random_part + common_row(key)[:, None] * beta_shift[None, :] * level_scale).astype(jnp.bfloat16)


def draw_decay_rate(key, part):
    slow_mask = slow_heads(key, slow_total())
    slow_rate = jnp.exp(jax.random.uniform(jax.random.fold_in(key, 6), (HEADS,), jnp.float32, math.log(0.2), math.log(0.6))) / (LONGEST * BLOCK_LEN)
    fast_rate = jnp.exp(jax.random.uniform(jax.random.fold_in(key, 7), (HEADS,), jnp.float32, math.log(0.003), math.log(0.05)))
    return (slow_mask * slow_rate + (1.0 - slow_mask) * fast_rate).astype(jnp.float32)


def draw_conv_value(key, part):
    slow_mask = slow_heads(key, slow_total())
    column_scale = jnp.repeat(0.5 + slow_mask, DV)
    random_part = unit_draw(jax.random.fold_in(key, 8), (CONV, HEADS * DV), 3.0)
    return (random_part * column_scale[None, :]).astype(jnp.float32)


def level_of(rng, shape, split, low, high):
    level, own = 1.0, jax.random.fold_in(rng, 6)
    for position, shards_of in split:
        heights = jnp.exp(jax.random.uniform(jax.random.fold_in(own, position), (shards_of,), jnp.float32, low / len(split), high / len(split)))
        level = level * jnp.repeat(heights, shape[position] // shards_of).reshape([-1 if axis == position else 1 for axis in range(len(shape))])
    return level


def length_profile(amount, total, limit, skew):
    portions = [(1 << 20) // math.isqrt(rank ** skew) + 1 for rank in range(2, amount + 1)]
    spare, given = total - limit - (amount - 1), [1] * (amount - 1)
    while spare > 0:
        free = [i for i in range(amount - 1) if given[i] < limit]
        whole, remaining = sum([portions[i] for i in free]), spare
        for i in free:
            addition = min(limit - given[i], max(1, remaining * portions[i] // whole), spare)
            given[i] = given[i] + addition
            spare = spare - addition
    return np.array([limit] + given)


def ragged(stream_key, number_of, total, reach, slope):
    if number_of == 2:
        one = jax.random.randint(stream_key, (), max(1, total - reach), min(reach, total - 1) + 1)
        return jnp.stack([one, total - one])
    sizes = jnp.asarray(length_profile(number_of, total, reach, slope), jnp.int32)
    twos = (number_of - 1) // 2
    donor, taker = sizes[1:1 + 2 * twos:2], sizes[2:2 + 2 * twos:2]
    margin = jnp.minimum(donor - 1, reach - taker)
    moved = jax.random.randint(jax.random.fold_in(stream_key, 1), (twos,), 0, 1 << 20) % (margin + 1)
    sizes = sizes.at[1:1 + 2 * twos:2].set(donor - moved).at[2:2 + 2 * twos:2].set(taker + moved)
    return sizes[jax.random.permutation(jax.random.fold_in(stream_key, 2), number_of)]


def noise(stream_key, extent, spread, most, pieces=(), kind=jnp.bfloat16):
    drawn = spread * jax.random.normal(stream_key, extent, jnp.float32)
    if pieces:
        drawn = drawn * level_of(stream_key, extent, pieces, -0.22, 0.18)
    return jnp.clip(drawn, -most, most).astype(kind)


def setup_inputs(seed: int = 0) -> dict:
    arg_keys = jax.random.split(jax.random.key(seed), 19)
    states_in = draw_states_in(jax.random.fold_in(arg_keys[18], 71), 0)
    lengths = ragged(arg_keys[1], REQUESTS, BLOCKS, LONGEST, 2).astype(jnp.int32)
    attn_gain = jnp.clip(1.0 + 0.1 * jax.random.normal(arg_keys[2], (D,), jnp.float32), 0.5, 1.5)
    w_query = noise(arg_keys[3], (D, HEADS * DK), D ** -0.5, 0.125, ((1, 4),))
    w_key = draw_w_key(jax.random.fold_in(arg_keys[18], 71), 0)
    w_value = noise(arg_keys[5], (D, HEADS * DV), D ** -0.5, 0.125, ((1, 4),))
    w_gate = noise(arg_keys[6], (D, HEADS * DV), D ** -0.5, 0.125, ((1, 4),))
    w_beta = draw_w_beta(jax.random.fold_in(arg_keys[18], 71), 0)
    w_alpha = noise(arg_keys[8], (D, HEADS), D ** -0.5, 0.125, ((1, 4),))
    decay_rate = draw_decay_rate(jax.random.fold_in(arg_keys[18], 71), 0)
    decay_bias = jnp.clip(-2.0 + 3.0 * jax.random.uniform(arg_keys[10], (HEADS,), jnp.float32) ** level_of(arg_keys[10], (HEADS,), ((0, 4),), -0.2, 0.2), -2.0, 1.0)
    conv_query = noise(arg_keys[11], (CONV, HEADS * DK), 0.5, 3.0, ((1, 4),), jnp.float32)
    conv_key = noise(arg_keys[12], (CONV, HEADS * DK), 0.5, 3.0, ((1, 4),), jnp.float32)
    conv_value = draw_conv_value(jax.random.fold_in(arg_keys[18], 71), 0)
    out_gain = jnp.clip(1.0 + 0.1 * jax.random.normal(arg_keys[14], (DV,), jnp.float32), 0.5, 1.5)
    w_out = noise(arg_keys[15], (HEADS * DV, D), (HEADS * DV) ** -0.5, 0.09375, ((0, 4),))
    final_gain = jnp.clip(1.0 + 0.1 * jax.random.normal(arg_keys[16], (D,), jnp.float32), 0.5, 1.5)
    w_head = noise(arg_keys[17], (D, VOCAB), 0.07, 0.41992188, ((1, 128),))
    return dict(states_in=states_in, lengths=lengths, attn_gain=attn_gain, w_query=w_query, w_key=w_key, w_value=w_value, w_gate=w_gate, w_beta=w_beta, w_alpha=w_alpha, decay_rate=decay_rate, decay_bias=decay_bias, conv_query=conv_query, conv_key=conv_key, conv_value=conv_value, out_gain=out_gain, w_out=w_out, final_gain=final_gain, w_head=w_head)


EPS = 1e-06
HIGH = lax.Precision.HIGHEST

def rms_scale(values, gain):
    return values * lax.rsqrt(lax.optimization_barrier(jnp.mean(values * values, axis=-1, keepdims=True)) + EPS) * gain

def unit_rows(values):
    return values * lax.rsqrt(lax.optimization_barrier(jnp.sum(values * values, axis=-1, keepdims=True)) + EPS)

def request_start(positions, offsets, block_len):
    block_ids = positions // block_len
    hits = offsets[None, :] <= block_ids[:, None]
    return block_len * lax.optimization_barrier(jnp.max(jnp.where(hits, offsets[None, :], 0), axis=1)).astype(jnp.int32)

def short_conv(extended, positions, start_tok, weight):
    row_count = positions.shape[0]
    tap_count = weight.shape[0]
    running = jnp.zeros((row_count, extended.shape[1]), jnp.float32)
    for tap_index in range(tap_count):
        lag_steps = tap_count - 1 - tap_index
        shifted = extended[tap_index:tap_index + row_count].astype(jnp.float32)
        valid = (positions - lag_steps >= start_tok)[:, None]
        running = running + jnp.where(valid, shifted, 0.0) * weight[tap_index]
    return jax.nn.silu(running)

def block_step(carry_state, block_inputs):
    q_rows, k_rows, v_rows, beta_rows, log_cum, keep_flag = block_inputs
    carry_state = carry_state * keep_flag
    block_len = q_rows.shape[1]
    row_ids = lax.broadcasted_iota(jnp.int32, (block_len, block_len), 0)
    col_ids = lax.broadcasted_iota(jnp.int32, (block_len, block_len), 1)
    on_lower = (row_ids >= col_ids).astype(jnp.float32)
    off_lower = (row_ids > col_ids).astype(jnp.float32)
    log_gap = log_cum[:, :, None] - log_cum[:, None, :]
    decays = jnp.exp(jnp.where(row_ids >= col_ids, log_gap, 0.0)) * on_lower
    growth = jnp.exp(log_cum)
    key_gram = jnp.einsum('hid,hjd->hij', k_rows, k_rows, precision=HIGH)
    system_mat = jnp.eye(block_len, dtype=jnp.float32) + beta_rows[:, :, None] * key_gram * decays * off_lower
    carried = jnp.einsum('hid,hde->hie', k_rows, carry_state, precision=HIGH)
    right_side = beta_rows[:, :, None] * (v_rows - growth[:, :, None] * carried)
    pseudo_values = lax.linalg.triangular_solve(system_mat, right_side, left_side=True, lower=True, unit_diagonal=True)
    scores = jnp.einsum('hid,hjd->hij', q_rows, k_rows, precision=HIGH) * decays
    output = growth[:, :, None] * jnp.einsum('hid,hde->hie', q_rows, carry_state, precision=HIGH)
    output = output + jnp.einsum('hij,hje->hie', scores, pseudo_values, precision=HIGH)
    tail_decay = jnp.exp(log_cum[:, -1:] - log_cum)
    carry_state = jnp.exp(log_cum[:, -1])[:, None, None] * carry_state + jnp.einsum('hjd,hje->hde', k_rows * tail_decay[:, :, None], pseudo_values, precision=HIGH)
    return (carry_state, (output, carry_state))

def to_blocks(values, block_count, head_count):
    return values.reshape(block_count, BLOCK_LEN, head_count, -1).transpose(0, 2, 1, 3)

def reference(states_in, lengths, attn_gain, w_query, w_key, w_value, w_gate, w_beta, w_alpha, decay_rate, decay_bias, conv_query, conv_key, conv_value, out_gain, w_out, final_gain, w_head):
    x_float = states_in.astype(jnp.float32)
    normed = rms_scale(x_float, attn_gain).astype(jnp.bfloat16)
    pre_q = jnp.dot(normed.astype(jnp.float32), w_query.astype(jnp.float32), preferred_element_type=jnp.float32).astype(jnp.bfloat16)
    pre_k = jnp.dot(normed.astype(jnp.float32), w_key.astype(jnp.float32), preferred_element_type=jnp.float32).astype(jnp.bfloat16)
    pre_v = jnp.dot(normed.astype(jnp.float32), w_value.astype(jnp.float32), preferred_element_type=jnp.float32).astype(jnp.bfloat16)
    gate_raw = jnp.dot(normed.astype(jnp.float32), w_gate.astype(jnp.float32), preferred_element_type=jnp.float32)
    beta_all = jax.nn.sigmoid(jnp.dot(normed.astype(jnp.float32), w_beta.astype(jnp.float32), preferred_element_type=jnp.float32))
    log_decay = -decay_rate * jax.nn.softplus(jnp.dot(normed.astype(jnp.float32), w_alpha.astype(jnp.float32), preferred_element_type=jnp.float32) + decay_bias)
    ends = jnp.cumsum(lengths).astype(jnp.int32)
    offsets = (ends - lengths).astype(jnp.int32)
    positions = jnp.arange(TOKENS, dtype=jnp.int32)
    start_tok = request_start(positions, offsets, BLOCK_LEN)
    edge_pad = jnp.zeros((CONV - 1, pre_q.shape[1]), jnp.bfloat16)
    conv_q = short_conv(jnp.concatenate([edge_pad, pre_q], axis=0), positions, start_tok, conv_query)
    conv_k = short_conv(jnp.concatenate([edge_pad, pre_k], axis=0), positions, start_tok, conv_key)
    value_pad = jnp.zeros((CONV - 1, pre_v.shape[1]), jnp.bfloat16)
    conv_v = short_conv(jnp.concatenate([value_pad, pre_v], axis=0), positions, start_tok, conv_value)
    q_heads = unit_rows(conv_q.reshape(TOKENS, HEADS, DK)) * DK ** (-0.5)
    k_heads = unit_rows(conv_k.reshape(TOKENS, HEADS, DK))
    q_blocks = to_blocks(q_heads, BLOCKS, HEADS)
    k_blocks = to_blocks(k_heads, BLOCKS, HEADS)
    v_blocks = to_blocks(conv_v, BLOCKS, HEADS)
    beta_blocks = beta_all.reshape(BLOCKS, BLOCK_LEN, HEADS).transpose(0, 2, 1)
    log_blocks = jnp.cumsum(log_decay.reshape(BLOCKS, BLOCK_LEN, HEADS).transpose(0, 2, 1), axis=2)
    block_ids = jnp.arange(BLOCKS, dtype=jnp.int32)
    keep_flags = 1.0 - lax.optimization_barrier(jnp.max((offsets[None, :] == block_ids[:, None]).astype(jnp.float32), axis=1))
    initial = jnp.zeros((HEADS, DK, DV), jnp.float32)
    last_state, (outputs, block_states) = lax.scan(block_step, initial, (q_blocks, k_blocks, v_blocks, beta_blocks, log_blocks, keep_flags))
    o_tokens = outputs.transpose(0, 2, 1, 3).reshape(TOKENS, HEADS, DV)
    gated = (rms_scale(o_tokens, out_gain) * jax.nn.silu(gate_raw.reshape(TOKENS, HEADS, DV))).astype(jnp.bfloat16)
    mixed = jnp.dot(gated.reshape(TOKENS, HEADS * DV).astype(jnp.float32), w_out.astype(jnp.float32), preferred_element_type=jnp.float32)
    hidden = (x_float + mixed).astype(jnp.bfloat16)
    last_rows = hidden[ends * BLOCK_LEN - 1].astype(jnp.float32)
    final = rms_scale(last_rows, final_gain).astype(jnp.bfloat16)
    logits = jnp.dot(final.astype(jnp.float32), w_head.astype(jnp.float32), preferred_element_type=jnp.float32)
    max_logit = lax.optimization_barrier(jnp.max(logits, axis=1))
    return (hidden, block_states, max_logit)
```

```python
import jax
import jax.numpy as jnp
from jax import lax
from jax.sharding import PartitionSpec as P

CONV = 4
BLOCK_LEN = 64
GROUP = 8
EPS = 1e-06
HIGH = lax.Precision.HIGHEST
F32 = jnp.float32
BF16 = jnp.bfloat16


def rms_scale(values, gain):
    return values * lax.rsqrt(jnp.mean(values * values, axis=-1, keepdims=True) + EPS) * gain


def unit_rows(values):
    return values * lax.rsqrt(jnp.sum(values * values, axis=-1, keepdims=True) + EPS)


def shift_groups(value, steps):
    count = lax.axis_size("seq")
    gap = steps * GROUP
    return lax.ppermute(value, "seq", [(source, source + gap) for source in range(count - gap)])


def group_exchange(value):
    count = lax.axis_size("seq")
    groups = [list(range(first, first + GROUP)) for first in range(0, count, GROUP)]
    return lax.all_to_all(value, "seq", 0, 0, axis_index_groups=groups)


def unit_lower_inverse(strict, size):
    rows = lax.broadcasted_iota(jnp.int32, (size, size), 0)
    cols = lax.broadcasted_iota(jnp.int32, (size, size), 1)
    mul = lambda a, b: jnp.einsum("...ij,...jk->...ik", a, b, precision=HIGH)
    eye = (rows == cols).astype(F32)
    within = strict * (rows // 8 == cols // 8)
    second = mul(within, within)
    fourth = mul(second, second)
    inverse = mul(mul(eye - within, eye + second), eye + fourth)
    width = 8
    while width < size:
        corner = strict * ((rows // (2 * width) == cols // (2 * width)) & (rows // width != cols // width))
        inverse = inverse - mul(mul(inverse, corner), inverse)
        width *= 2
    return inverse


def local_maps(q, k, v, beta, log_decay, keep):
    mul = lambda spec, a, b: jnp.einsum(spec, a, b, precision=HIGH)
    size = q.shape[2]
    rows = lax.broadcasted_iota(jnp.int32, (size, size), 0)
    cols = lax.broadcasted_iota(jnp.int32, (size, size), 1)
    log_cum = jnp.cumsum(log_decay, axis=2)
    gap = log_cum[..., :, None] - log_cum[..., None, :]
    decays = jnp.exp(jnp.where(rows >= cols, gap, 0.0)) * (rows >= cols)
    growth = jnp.exp(log_cum)[..., None]
    strict = beta[..., None] * mul("bhid,bhjd->bhij", k, k) * decays * (rows > cols)
    inverse = unit_lower_inverse(strict, size)
    w = mul("bhij,bhjd->bhid", inverse, beta[..., None] * growth * k)
    u = mul("bhij,bhjd->bhid", inverse, beta[..., None] * v)
    scores = mul("bhid,bhjd->bhij", q, k) * decays
    q_eff = growth * q - mul("bhij,bhjd->bhid", scores, w)
    o_own = mul("bhij,bhjd->bhid", scores, u)
    tail = jnp.exp(log_cum[..., -1:] - log_cum)[..., None] * k
    last = jnp.exp(log_cum[..., -1])[..., None, None]
    eye = jnp.eye(k.shape[-1], dtype=F32)
    step_a = last * eye - mul("bhjd,bhje->bhde", tail, w)
    step_b = mul("bhjd,bhje->bhde", tail, u)
    a_run = jnp.broadcast_to(eye, step_a.shape[1:])
    b_run = jnp.zeros_like(step_b[0])
    a_list, b_list, qa_list, o_list = [], [], [], []
    for block in range(q.shape[0]):
        a_run = a_run * keep[block]
        b_run = b_run * keep[block]
        qa_list.append(mul("hid,hde->hie", q_eff[block], a_run))
        o_list.append(mul("hid,hde->hie", q_eff[block], b_run) + o_own[block])
        a_run = mul("hid,hde->hie", step_a[block], a_run)
        b_run = mul("hid,hde->hie", step_a[block], b_run) + step_b[block]
        a_list.append(a_run)
        b_list.append(b_run)
    return [jnp.stack(x) for x in (a_list, b_list, qa_list, o_list)]


def pack_map(a, b):
    size = a.shape[-1]
    eye = jnp.eye(size, dtype=F32)
    diag = jnp.sum(a * eye, axis=-2)
    high = diag.astype(BF16)
    low = (diag - high.astype(F32)).astype(BF16)
    pad = jnp.zeros(a.shape[:-2] + (14, size), BF16)
    return jnp.concatenate(
        [(a - a * eye).astype(BF16), high[..., None, :], low[..., None, :], pad, b.astype(BF16)], axis=-2
    )


def unpack_map(packed):
    size = packed.shape[-1]
    eye = jnp.eye(size, dtype=F32)
    wide = packed.astype(F32)
    diag = wide[..., size : size + 1, :] + wide[..., size + 1 : size + 2, :]
    return wide[..., :size, :] + eye * diag, wide[..., size + 16 :, :]


def to_blocks(values, block_count, head_count):
    return values.reshape(block_count, BLOCK_LEN, head_count, -1).transpose(0, 2, 1, 3)


def body(
    states_in, lengths, attn_gain, w_query, w_key, w_value, w_gate, w_beta, w_alpha, decay_rate,
    decay_bias, conv_query, conv_key, conv_value, out_gain, w_out, final_gain, w_head,
):
    mul = lambda spec, a, b: jnp.einsum(spec, a, b, precision=HIGH)
    tok = states_in.shape[0]
    heads = decay_rate.shape[0]
    dk = w_query.shape[1] // heads
    dv = w_value.shape[1] // heads
    blocks = tok // BLOCK_LEN
    seq_count = lax.axis_size("seq")
    tp_count = lax.axis_size("tp")
    piece = lax.axis_index("seq")
    shard = lax.axis_index("tp")
    model = states_in.shape[1]
    share = model // tp_count

    halo = lax.ppermute(states_in[tok - 8 :], "seq", [(i, i + 1) for i in range(seq_count - 1)])
    x_ext = jnp.concatenate([halo, states_in], axis=0).astype(F32)
    normed_ext = rms_scale(x_ext, attn_gain).astype(BF16)
    normed = normed_ext[8:]
    dot = lambda a, b: jnp.dot(a, b, preferred_element_type=F32)
    pre = jnp.concatenate([dot(normed_ext, w) for w in (w_query, w_key, w_value)], axis=1).astype(BF16)
    gate_raw = dot(normed, w_gate)
    beta = jax.nn.sigmoid(dot(normed, w_beta))
    log_decay = -decay_rate * jax.nn.softplus(dot(normed, w_alpha) + decay_bias)

    ends = jnp.cumsum(lengths)
    offsets = ends - lengths
    block_ids = piece * blocks + jnp.arange(blocks, dtype=jnp.int32)
    keep = 1.0 - jnp.max((offsets[None, :] == block_ids[:, None]).astype(F32), axis=1)

    taps = jnp.concatenate([conv_query, conv_key, conv_value], axis=1)
    in_block = jnp.arange(tok, dtype=jnp.int32) % BLOCK_LEN
    keep_rows = jnp.repeat(keep, BLOCK_LEN) > 0.5
    conv = jnp.zeros((tok, pre.shape[1]), F32)
    for tap in range(CONV):
        lag = CONV - 1 - tap
        rows = pre[8 - lag : 8 - lag + tok].astype(F32)
        valid = (keep_rows | (in_block >= lag))[:, None]
        conv = conv + jnp.where(valid, rows, 0.0) * taps[tap]
    conv = jax.nn.silu(conv)
    qk = heads * dk
    q = unit_rows(conv[:, :qk].reshape(tok, heads, dk)) * dk ** (-0.5)
    k = unit_rows(conv[:, qk : 2 * qk].reshape(tok, heads, dk))
    qb = to_blocks(q, blocks, heads)
    kb = to_blocks(k, blocks, heads)
    vb = to_blocks(conv[:, 2 * qk :], blocks, heads)
    beta_b = beta.reshape(blocks, BLOCK_LEN, heads).transpose(0, 2, 1)
    log_b = log_decay.reshape(blocks, BLOCK_LEN, heads).transpose(0, 2, 1)
    a_all, b_all, qa, o_own = local_maps(qb, kb, vb, beta_b, log_b, keep)

    half = dv // 2
    halves = b_all[-1].reshape(heads, dk, 2, half).transpose(0, 2, 1, 3)
    maps = pack_map(jnp.broadcast_to(a_all[-1][:, None], (heads, 2, dk, dk)), halves)
    got = group_exchange(maps.reshape(heads * 2, -1, dk))
    a_got, b_got = unpack_map(got)
    run = jnp.concatenate([jnp.eye(dk, dtype=F32), jnp.zeros((dk, half), F32)], axis=1)
    before = []
    for member in range(GROUP):
        before.append(run)
        run = mul("de,ef->df", a_got[member], run)
        run = run.at[:, dk:].add(b_got[member])
    total = pack_map(run[:, :dk], run[:, dk:])
    one_back = shift_groups(total, 1)
    two_back = shift_groups(total[dk + 16 :], 2)
    a_one, b_one = unpack_map(one_back)
    entering = mul("de,ef->df", a_one, two_back.astype(F32)) + b_one
    before = jnp.stack(before)
    incoming = mul("pde,ef->pdf", before[:, :, :dk], entering) + before[:, :, dk:]
    back = group_exchange(incoming.astype(BF16))
    s_in = back.reshape(heads, 2, dk, half).transpose(0, 2, 1, 3).reshape(heads, dk, dv).astype(F32)

    o_blocks = mul("bhcd,hde->bhce", qa, s_in) + o_own
    block_states = mul("bhde,hef->bhdf", a_all, s_in) + b_all
    o_tok = o_blocks.transpose(0, 2, 1, 3).reshape(tok, heads, dv)
    gated = (rms_scale(o_tok, out_gain) * jax.nn.silu(gate_raw.reshape(tok, heads, dv))).astype(BF16)
    gated = gated.reshape(tok, heads * dv)

    positions = piece * tok + jnp.arange(tok, dtype=jnp.int32)
    picker = ((ends * BLOCK_LEN - 1)[:, None] == positions[None, :]).astype(BF16)
    x_own = lax.dynamic_slice_in_dim(states_in, shard * share, share, 1)
    picked = dot(picker, jnp.concatenate([gated, x_own], axis=1)).astype(BF16)
    rows_all = lax.all_to_all(jnp.broadcast_to(picked[None], (seq_count,) + picked.shape), "seq", 0, 0)
    rows = jnp.sum(rows_all.astype(F32), axis=0).astype(BF16)

    parts = dot(gated, w_out).reshape(tok, tp_count, share)
    take = lambda offset: lax.dynamic_index_in_dim(parts, (shard + offset) % tp_count, 1, keepdims=False)
    mixed = take(0)
    for offset in range(1, tp_count):
        ring = [(i, (i + offset) % tp_count) for i in range(tp_count)]
        mixed = mixed + lax.ppermute(take(offset).astype(BF16), "tp", ring).astype(F32)
    hidden = (x_own.astype(F32) + mixed).astype(BF16)

    row_parts = dot(rows[:, : heads * dv], w_out)
    row_parts = lax.dynamic_update_slice_in_dim(
        row_parts,
        lax.dynamic_slice_in_dim(row_parts, shard * share, share, 1) + rows[:, heads * dv :].astype(F32),
        shard * share,
        1,
    )
    last = lax.psum(row_parts, "tp").astype(BF16).astype(F32)
    final = rms_scale(last, final_gain).astype(BF16)
    best = jnp.max(dot(final, w_head), axis=1)
    spread = jnp.broadcast_to(jnp.pad(best, (0, 124))[None, None], (seq_count * tp_count, 1, 128))
    bests = lax.all_to_all(spread, ("seq", "tp"), 0, 0)
    max_logit = jnp.max(bests[:, 0, :4], axis=0)
    return (hidden, block_states, max_logit)


def solution(mesh):
    return jax.shard_map(
        body,
        mesh=mesh,
        in_specs=(
            P("seq", None), P(), P(), P(None, "tp"), P(None, "tp"), P(None, "tp"), P(None, "tp"),
            P(None, "tp"), P(None, "tp"), P("tp"), P("tp"), P(None, "tp"), P(None, "tp"), P(None, "tp"),
            P(), P("tp", None), P(), P(None, ("seq", "tp")),
        ),
        out_specs=(P("seq", "tp"), P("seq", "tp", None, None), P()),
        check_vma=False,
    )
```

```python
import functools

import jax
import jax.numpy as jnp
from jax import lax
from jax.experimental import pallas as pl
from jax.experimental.pallas import tpu as pltpu
from jax.sharding import PartitionSpec as P

CONV = 4
BLOCK_LEN = 64
GROUP = 8
HALO = 16
PAD = 16
EPS = 1e-06
HIGH = lax.Precision.HIGHEST
F32 = jnp.float32
BF16 = jnp.bfloat16

VMEM = pl.BlockSpec(memory_space=pltpu.VMEM)
SMEM = pl.BlockSpec(memory_space=pltpu.SMEM)


def rms_scale(values, gain):
    return values * lax.rsqrt(jnp.mean(values * values, axis=-1, keepdims=True) + EPS) * gain


def shift_groups(value, steps):
    count = lax.axis_size("seq")
    gap = steps * GROUP
    return lax.ppermute(value, "seq", [(source, source + gap) for source in range(count - gap)])


def group_exchange(value):
    count = lax.axis_size("seq")
    groups = [list(range(first, first + GROUP)) for first in range(0, count, GROUP)]
    return lax.all_to_all(value, "seq", 0, 0, axis_index_groups=groups)


def dot(a, b):
    return jnp.dot(a, b, preferred_element_type=F32)


def dot_nt(a, b):
    return lax.dot_general(a, b, (((1,), (1,)), ((), ())), preferred_element_type=F32)


def dot_tn(a, b):
    return lax.dot_general(a, b, (((0,), (0,)), ((), ())), preferred_element_type=F32)


def split(a):
    high = a.astype(BF16)
    return high, (a - high.astype(F32)).astype(BF16)


def dot3(a, b):
    a_high, a_low = split(a)
    b_high, b_low = split(b)
    return dot(a_high, b_high) + dot(a_high, b_low) + dot(a_low, b_high)


def iotas(rows, cols):
    return (
        lax.broadcasted_iota(jnp.int32, (rows, cols), 0),
        lax.broadcasted_iota(jnp.int32, (rows, cols), 1),
    )


def gate_kernel(x_ref, gain_ref, w_gate_ref, wb_ref, wa_ref, rate_ref, bias_ref, normed_ref, gate_ref, scal_ref):
    tok = x_ref.shape[0]
    heads = wb_ref.shape[0]
    normed_ref[...] = rms_scale(x_ref[...].astype(F32), gain_ref[...]).astype(BF16)
    normed = normed_ref[...]
    beta = jax.nn.sigmoid(dot_nt(normed, wb_ref[...]))
    raw = dot_nt(normed, wa_ref[...]) + bias_ref[...]
    soft = jnp.maximum(raw, 0.0) + jnp.log1p(jnp.exp(-jnp.abs(raw)))
    log_decay = -rate_ref[...] * soft
    rows, cols = iotas(tok, tok)
    same = rows // BLOCK_LEN == cols // BLOCK_LEN
    run = jnp.dot((same & (rows >= cols)).astype(F32), log_decay, precision=HIGH, preferred_element_type=F32)
    full = jnp.dot(same.astype(F32), log_decay, precision=HIGH, preferred_element_type=F32)
    for place, value in enumerate((beta, run, jnp.exp(run), jnp.exp(full - run), jnp.exp(full))):
        scal_ref[:, place * heads : (place + 1) * heads] = value
    gate_ref[...] = jax.nn.silu(dot(normed, w_gate_ref[...]))


def unit_lower_inverse(packed, spread, rows, cols):
    eye = (rows == cols).astype(F32)
    within = jnp.where(rows // 8 == cols // 8, packed, 0.0)
    second = dot3(within, spread(within))
    fourth = dot3(second, spread(second))
    inverse = dot3(eye - within, spread(eye + second))
    inverse = dot3(inverse, spread(eye + fourth))
    width = 8
    while width < BLOCK_LEN:
        corner = jnp.where((rows // (2 * width) == cols // (2 * width)) & (rows // width != cols // width), packed, 0.0)
        inverse = inverse - dot3(dot3(inverse, spread(corner)), spread(inverse))
        width *= 2
    return inverse


def store_map(ref, at, a, b, eye):
    size = a.shape[0]
    diag = jnp.sum(jnp.where(eye, a, 0.0), axis=0, keepdims=True)
    high = diag.astype(BF16).astype(F32)
    low = diag - high
    place = lax.broadcasted_iota(jnp.int32, (PAD, size), 0)
    ref[at, :size, :] = jnp.where(eye, 0.0, a).astype(BF16)
    ref[at, size : size + PAD, :] = jnp.where(place == 0, high, jnp.where(place == 1, low, 0.0)).astype(BF16)
    ref[at, size + PAD :, :] = b.astype(BF16)


def load_map(value, eye):
    size = value.shape[1]
    diag = value[size : size + PAD].astype(F32)
    a = value[:size].astype(F32) + jnp.where(eye, diag[0:1] + diag[1:2], 0.0)
    return a, value[size + PAD :].astype(F32)


def maps_kernel(
    meta_ref, normed_ref, halo_ref, gain_ref, wq_ref, wk_ref, wv_ref, tq_ref, tk_ref, tv_ref, scal_ref,
    maps_ref, qa_ref, own_ref, a_ref, b_ref, lhs, pre, qs, ks, vs,
):
    tok = normed_ref.shape[0]
    blocks = tok // BLOCK_LEN
    heads = qa_ref.shape[0]
    dk = qa_ref.shape[2]
    dv = own_ref.shape[2]
    rows_all = heads * BLOCK_LEN
    keep = []
    first_block = meta_ref[REQ] * blocks
    for block in range(blocks):
        offset = jnp.int32(0)
        flag = jnp.float32(1.0)
        for request in range(REQ):
            flag = jnp.where(offset == first_block + block, 0.0, flag)
            offset = offset + meta_ref[request]
        keep.append(flag)
    lhs[:HALO, :] = rms_scale(halo_ref[...].astype(F32), gain_ref[...]).astype(BF16)
    lhs[HALO:, :] = normed_ref[...]
    qk = heads * dk
    pre[:, :qk] = dot(lhs[...], wq_ref[...]).astype(BF16).astype(F32)
    pre[:, qk : 2 * qk] = dot(lhs[...], wk_ref[...]).astype(BF16).astype(F32)
    pre[:, 2 * qk :] = dot(lhs[...], wv_ref[...]).astype(BF16).astype(F32)
    token = lax.broadcasted_iota(jnp.int32, (tok, 1), 0)
    masks = {}
    for lag in range(1, CONV):
        mask = jnp.ones((tok, 1), F32)
        for block in range(blocks):
            start = block * BLOCK_LEN
            mask = jnp.where((token >= start) & (token < start + lag), keep[block], mask)
        masks[lag] = mask

    def conv(first, taps_ref, at):
        total = None
        for tap in range(CONV):
            lag = CONV - 1 - tap
            part = pre[HALO - lag : HALO - lag + tok, first : first + dk] * taps_ref[tap : tap + 1, at : at + dk]
            if lag:
                part = part * masks[lag]
            total = part if total is None else total + part
        return jax.nn.silu(total)

    for head in range(heads):
        low = head * BLOCK_LEN
        for ref, base, taps_ref, scale in ((qs, 0, tq_ref, dk ** (-0.5)), (ks, qk, tk_ref, 1.0)):
            value = conv(base + head * dk, taps_ref, head * dk)
            value = value * (lax.rsqrt(jnp.sum(value * value, axis=-1, keepdims=True) + EPS) * scale)
            for block in range(blocks):
                ref[block, low : low + BLOCK_LEN, :] = value[block * BLOCK_LEN : (block + 1) * BLOCK_LEN]
        for part in range(dv // dk):
            at = head * dv + part * dk
            value = conv(2 * qk + at, tv_ref, at)
            for block in range(blocks):
                vs[block, low : low + BLOCK_LEN, part * dk : (part + 1) * dk] = value[
                    block * BLOCK_LEN : (block + 1) * BLOCK_LEN
                ]

    rows, cols = iotas(rows_all, rows_all)
    same = rows // BLOCK_LEN == cols // BLOCK_LEN
    lower = same & (rows >= cols)
    strict = same & (rows > cols)
    diagonal = rows == cols
    p_rows, p_cols = iotas(BLOCK_LEN, rows_all)
    p_cols = p_cols % BLOCK_LEN
    spread = lambda value: jnp.where(same, jnp.concatenate([value] * heads, axis=0), 0.0)
    k_rows, k_cols = iotas(dk, dk)
    eye = k_rows == k_cols

    def column(place, block):
        span = slice(block * BLOCK_LEN, (block + 1) * BLOCK_LEN)
        at = place * heads
        return jnp.concatenate([scal_ref[span, at + head : at + head + 1] for head in range(heads)], axis=0)

    q_effs, owns, tails, wus = [], [], [], []
    for block in range(blocks):
        q, k, v = qs[block], ks[block], vs[block]
        kb = k.astype(BF16)
        beta = column(0, block)
        run = column(1, block)
        growth = column(2, block)
        across = jnp.sum(jnp.where(diagonal, run, 0.0), axis=0, keepdims=True)
        decays = jnp.where(lower, jnp.exp(jnp.where(lower, run - across, 0.0)), 0.0)
        system = jnp.where(strict, beta * dot_nt(kb, kb) * decays, 0.0)
        packed = system[:BLOCK_LEN]
        for head in range(1, heads):
            packed = packed + system[head * BLOCK_LEN : (head + 1) * BLOCK_LEN]
        inverse = spread(unit_lower_inverse(packed, spread, p_rows, p_cols)).astype(BF16)
        right = jnp.concatenate([(beta * growth) * k, beta * v], axis=1).astype(BF16)
        wu = dot(inverse, right).astype(BF16)
        scores = (dot_nt(q.astype(BF16), kb) * decays).astype(BF16)
        mixed = dot(scores, wu)
        q_effs.append((growth * q - mixed[:, :dk]).astype(BF16))
        owns.append(mixed[:, dk:])
        tails.append((column(3, block) * k).astype(BF16))
        wus.append(wu)

    for head in range(heads):
        span = slice(head * BLOCK_LEN, (head + 1) * BLOCK_LEN)
        a_run = b_run = None
        for block in range(blocks):
            there = slice(block * BLOCK_LEN, (block + 1) * BLOCK_LEN)
            grown = dot_tn(tails[block][span], wus[block][span])
            last = scal_ref[block * BLOCK_LEN : block * BLOCK_LEN + 1, 4 * heads + head : 4 * heads + head + 1]
            shrink, add = grown[:, :dk], grown[:, dk:]
            if block == 0:
                qa_ref[head, there, :] = (q_effs[block][span].astype(F32) * keep[0]).astype(BF16)
                own_ref[head, there, :] = owns[block][span]
                a_run = (jnp.where(eye, last, 0.0) - shrink) * keep[0]
                b_run = add
            else:
                joint = jnp.concatenate([a_run, b_run], axis=1) * keep[block]
                joint_b = joint.astype(BF16)
                seen = dot(q_effs[block][span], joint_b)
                qa_ref[head, there, :] = seen[:, :dk].astype(BF16)
                own_ref[head, there, :] = seen[:, dk:] + owns[block][span]
                joint = last * joint - dot(shrink.astype(BF16), joint_b)
                a_run = joint[:, :dk]
                b_run = joint[:, dk:] + add
            a_ref[block, head] = a_run
            b_ref[block, head] = b_run
        for part in range(2):
            store_map(maps_ref, 2 * head + part, a_run, b_run[:, part * dk : (part + 1) * dk], eye)


def scan_kernel(got_ref, before_ref, total_ref):
    size = got_ref.shape[2]
    rows, cols = iotas(size, size)
    eye = rows == cols
    run = None
    for member in range(GROUP):
        a, b = load_map(got_ref[member], eye)
        if run is None:
            before_ref[member] = jnp.concatenate([eye.astype(F32), jnp.zeros((size, size), F32)], axis=1)
            run = jnp.concatenate([a, b], axis=1)
        else:
            before_ref[member] = run
            run = dot3(a, run)
            run = jnp.concatenate([run[:, :size], run[:, size:] + b], axis=1)
    store_map(total_ref, 0, run[:, :size], run[:, size:], eye)


def apply_kernel(one_ref, two_ref, before_ref, out_ref):
    size = one_ref.shape[2]
    rows, cols = iotas(size, size)
    eye = rows == cols
    a, b = load_map(one_ref[0], eye)
    a_high, a_low = split(a)
    entering = dot(a_high, two_ref[...]) + dot(a_low, two_ref[...]) + b
    e_high, e_low = split(entering)
    for member in range(GROUP):
        p_high, p_low = split(before_ref[member, :, :size])
        value = dot(p_high, e_high) + dot(p_high, e_low) + dot(p_low, e_high) + before_ref[member, :, size:]
        out_ref[member] = value.astype(BF16)


def output_kernel(meta_ref, s_ref, qa_ref, own_ref, gate_ref, gain_ref, x_ref, gated_ref, rows_ref):
    heads, tok, dk = qa_ref.shape
    dv = own_ref.shape[2]
    width = heads * dv
    for head in range(heads):
        state = jnp.concatenate([s_ref[2 * head], s_ref[2 * head + 1]], axis=1)
        out = dot(qa_ref[head], state) + own_ref[head]
        span = slice(head * dv, (head + 1) * dv)
        gated_ref[:, span] = (rms_scale(out, gain_ref[...]) * gate_ref[:, span]).astype(BF16)
    place, token = iotas(rows_ref.shape[0], tok)
    first = meta_ref[REQ] * tok
    end = jnp.int32(0)
    picker = jnp.zeros(place.shape, F32)
    for request in range(REQ):
        end = end + meta_ref[request]
        picker = jnp.where((place == request) & (token + first == end * BLOCK_LEN - 1), 1.0, picker)
    picker = picker.astype(BF16)
    rows_ref[:, :width] = dot(picker, gated_ref[...]).astype(BF16)
    rows_ref[:, width:] = dot(picker, x_ref[...]).astype(BF16)


def mix_kernel(meta_ref, gated_ref, w_ref, x_ref, away_ref, here_ref):
    step = pl.program_id(0)
    value = dot(gated_ref[...], w_ref[...])
    away_ref[0] = value.astype(BF16)

    @pl.when(step == pl.num_programs(0) - 1)
    def _():
        here_ref[...] = value + x_ref[...].astype(F32)


def states_kernel(a_ref, b_ref, s_ref, out_ref):
    heads = a_ref.shape[1]
    for head in range(heads):
        state = jnp.concatenate([s_ref[2 * head], s_ref[2 * head + 1]], axis=1)
        high, low = split(a_ref[0, head])
        out_ref[0, head] = dot(high, state) + dot(low, state) + b_ref[0, head]


REQ = 4


def body(
    states_in, lengths, attn_gain, w_query, w_key, w_value, w_gate, w_beta, w_alpha, decay_rate,
    decay_bias, conv_query, conv_key, conv_value, out_gain, w_out, final_gain, w_head,
):
    tok, model = states_in.shape
    heads = decay_rate.shape[0]
    dk = w_query.shape[1] // heads
    dv = w_value.shape[1] // heads
    blocks = tok // BLOCK_LEN
    seq_count = lax.axis_size("seq")
    tp_count = lax.axis_size("tp")
    piece = lax.axis_index("seq")
    shard = lax.axis_index("tp")
    share = model // tp_count
    rows_all = heads * BLOCK_LEN
    shape = jax.ShapeDtypeStruct
    params = lambda mib: pltpu.CompilerParams(vmem_limit_bytes=mib << 20)
    meta = jnp.concatenate([lengths, piece[None], shard[None]]).astype(jnp.int32)

    halo = lax.ppermute(states_in[tok - HALO :], "seq", [(i, i + 1) for i in range(seq_count - 1)])
    gain = attn_gain[None, :]
    normed, gate, scal = pl.pallas_call(
        gate_kernel,
        out_shape=(shape((tok, model), BF16), shape((tok, heads * dv), F32), shape((tok, 128), F32)),
        in_specs=[VMEM] * 7,
        out_specs=(VMEM,) * 3,
        compiler_params=params(24),
        name="gate_kernel",
    )(states_in, gain, w_gate, w_beta.T, w_alpha.T, decay_rate[None, :], decay_bias[None, :])

    maps, qa, own, a_all, b_all = pl.pallas_call(
        maps_kernel,
        out_shape=(
            shape((2 * heads, 2 * dk + PAD, dk), BF16),
            shape((heads, tok, dk), BF16),
            shape((heads, tok, dv), F32),
            shape((blocks, heads, dk, dk), F32),
            shape((blocks, heads, dk, dv), F32),
        ),
        in_specs=[SMEM] + [VMEM] * 10,
        out_specs=(VMEM,) * 5,
        scratch_shapes=[
            pltpu.VMEM((HALO + tok, model), BF16),
            pltpu.VMEM((HALO + tok, 2 * heads * dk + heads * dv), F32),
            pltpu.VMEM((blocks, rows_all, dk), F32),
            pltpu.VMEM((blocks, rows_all, dk), F32),
            pltpu.VMEM((blocks, rows_all, dv), F32),
        ],
        compiler_params=params(40),
        name="maps_kernel",
    )(meta, normed, halo, gain, w_query, w_key, w_value, conv_query, conv_key, conv_value, scal)

    got = group_exchange(maps)
    before, total = pl.pallas_call(
        scan_kernel,
        out_shape=(shape((GROUP, dk, 2 * dk), F32), shape((1, 2 * dk + PAD, dk), BF16)),
        in_specs=[VMEM],
        out_specs=(VMEM,) * 2,
        compiler_params=params(16),
        name="scan_kernel",
    )(got)
    one_back = shift_groups(total, 1)
    two_back = shift_groups(total[0, dk + PAD :], 2)
    incoming = pl.pallas_call(
        apply_kernel,
        out_shape=shape((GROUP, dk, dk), BF16),
        in_specs=[VMEM] * 3,
        out_specs=VMEM,
        compiler_params=params(16),
        name="apply_kernel",
    )(one_back, two_back, before)
    s_in = group_exchange(incoming)

    gated, picked = pl.pallas_call(
        output_kernel,
        out_shape=(shape((tok, heads * dv), BF16), shape((REQ, heads * dv + share), BF16)),
        grid_spec=pltpu.PrefetchScalarGridSpec(
            num_scalar_prefetch=1,
            grid=(1,),
            in_specs=[
                pl.BlockSpec((2 * heads, dk, dk), lambda i, m: (0, 0, 0)),
                pl.BlockSpec((heads, tok, dk), lambda i, m: (0, 0, 0)),
                pl.BlockSpec((heads, tok, dv), lambda i, m: (0, 0, 0)),
                pl.BlockSpec((tok, heads * dv), lambda i, m: (0, 0)),
                pl.BlockSpec((1, dv), lambda i, m: (0, 0)),
                pl.BlockSpec((tok, share), lambda i, m: (0, m[REQ + 1])),
            ],
            out_specs=(
                pl.BlockSpec((tok, heads * dv), lambda i, m: (0, 0)),
                pl.BlockSpec((REQ, heads * dv + share), lambda i, m: (0, 0)),
            ),
        ),
        compiler_params=params(24),
        name="output_kernel",
    )(meta, s_in, qa, own, gate, out_gain[None, :], states_in)

    rows_all_pieces = lax.all_to_all(jnp.broadcast_to(picked[None], (seq_count,) + picked.shape), "seq", 0, 0)

    turn = lambda i, m: (m[REQ + 1] + i + 1) % tp_count
    away, here = pl.pallas_call(
        mix_kernel,
        out_shape=(shape((tp_count, tok, share), BF16), shape((tok, share), F32)),
        grid_spec=pltpu.PrefetchScalarGridSpec(
            num_scalar_prefetch=1,
            grid=(tp_count,),
            in_specs=[
                pl.BlockSpec((tok, heads * dv), lambda i, m: (0, 0)),
                pl.BlockSpec((heads * dv, share), lambda i, m: (0, turn(i, m))),
                pl.BlockSpec((tok, share), lambda i, m: (0, m[REQ + 1])),
            ],
            out_specs=(
                pl.BlockSpec((1, tok, share), lambda i, m: (i, 0, 0)),
                pl.BlockSpec((tok, share), lambda i, m: (0, 0)),
            ),
        ),
        compiler_params=params(24),
        name="mix_kernel",
    )(meta, gated, w_out, states_in)
    mixed = here
    for offset in range(1, tp_count):
        ring = [(i, (i + offset) % tp_count) for i in range(tp_count)]
        mixed = mixed + lax.ppermute(away[offset - 1], "tp", ring).astype(F32)
    hidden = mixed.astype(BF16)

    block_states = pl.pallas_call(
        states_kernel,
        out_shape=shape((blocks, heads, dk, dv), F32),
        grid=(blocks,),
        in_specs=[
            pl.BlockSpec((1, heads, dk, dk), lambda i: (i, 0, 0, 0)),
            pl.BlockSpec((1, heads, dk, dv), lambda i: (i, 0, 0, 0)),
            pl.BlockSpec((2 * heads, dk, dk), lambda i: (0, 0, 0)),
        ],
        out_specs=pl.BlockSpec((1, heads, dk, dv), lambda i: (i, 0, 0, 0)),
        compiler_params=params(16),
        name="states_kernel",
    )(a_all, b_all, s_in)

    rows = jnp.sum(rows_all_pieces.astype(F32), axis=0).astype(BF16)
    row_parts = dot(rows[:, : heads * dv], w_out)
    row_parts = lax.dynamic_update_slice_in_dim(
        row_parts,
        lax.dynamic_slice_in_dim(row_parts, shard * share, share, 1) + rows[:, heads * dv :].astype(F32),
        shard * share,
        1,
    )
    last = lax.psum(row_parts, "tp").astype(BF16).astype(F32)
    final = rms_scale(last, final_gain).astype(BF16)
    best = jnp.max(dot(final, w_head), axis=1)
    spread = jnp.broadcast_to(jnp.pad(best, (0, 124))[None, None], (seq_count * tp_count, 1, 128))
    bests = lax.all_to_all(spread, ("seq", "tp"), 0, 0)
    max_logit = jnp.max(bests[:, 0, :4], axis=0)
    return (hidden, block_states, max_logit)


def solution(mesh):
    return jax.shard_map(
        body,
        mesh=mesh,
        in_specs=(
            P("seq", None), P(), P(), P(None, "tp"), P(None, "tp"), P(None, "tp"), P(None, "tp"),
            P(None, "tp"), P(None, "tp"), P("tp"), P("tp"), P(None, "tp"), P(None, "tp"), P(None, "tp"),
            P(), P("tp", None), P(), P(None, ("seq", "tp")),
        ),
        out_specs=(P("seq", "tp"), P("seq", "tp", None, None), P()),
        check_vma=False,
    )
```

```python
import jax
import jax.numpy as jnp
from jax import lax
from jax.experimental import pallas as pl
from jax.experimental.pallas import tpu as pltpu
from jax.sharding import PartitionSpec as P


CONV = 4
BLOCK_LEN = 64
GROUP = 8
HALO = 16
PAD = 16
EPS = 1e-06
HIGH = lax.Precision.HIGHEST
F32 = jnp.float32
BF16 = jnp.bfloat16

VMEM = pl.BlockSpec(memory_space=pltpu.VMEM)
HBM = pl.BlockSpec(memory_space=pltpu.HBM)
SMEM = pl.BlockSpec(memory_space=pltpu.SMEM)


def whole(*dims):
    return pl.BlockSpec(dims, lambda *_: (0,) * len(dims))


def hbm(*values):
    return [pltpu.with_memory_space_constraint(value, pltpu.HBM) for value in values]


def rms_scale(values, gain):
    return values * lax.rsqrt(jnp.mean(values * values, axis=-1, keepdims=True) + EPS) * gain


def shift_groups(value, steps):
    count = lax.axis_size("seq")
    gap = steps * GROUP
    return lax.ppermute(value, "seq", [(source, source + gap) for source in range(count - gap)])


def group_exchange(value):
    count = lax.axis_size("seq")
    groups = [list(range(first, first + GROUP)) for first in range(0, count, GROUP)]
    return lax.all_to_all(value, "seq", 0, 0, axis_index_groups=groups)


def dot(a, b):
    return jnp.dot(a, b, preferred_element_type=F32)


def dot_nt(a, b):
    return lax.dot_general(a, b, (((1,), (1,)), ((), ())), preferred_element_type=F32)


def dot_tn(a, b):
    return lax.dot_general(a, b, (((0,), (0,)), ((), ())), preferred_element_type=F32)


def split(a):
    high = a.astype(BF16)
    return high, (a - high.astype(F32)).astype(BF16)


def dot3(a, b):
    a_high, a_low = split(a)
    b_high, b_low = split(b)
    return dot(a_high, b_high) + dot(a_high, b_low) + dot(a_low, b_high)


def iotas(rows, cols):
    return (
        lax.broadcasted_iota(jnp.int32, (rows, cols), 0),
        lax.broadcasted_iota(jnp.int32, (rows, cols), 1),
    )


def last_blocks(meta_ref):
    place = lax.broadcasted_iota(jnp.int32, (REQ, 1), 0)
    final = jnp.zeros((REQ, 1), jnp.int32)
    end = jnp.int32(0)
    for request in range(REQ):
        end = end + meta_ref[request]
        final = jnp.where(place == request, end - 1, final)
    return final


def norm_kernel(x_ref, gain_ref, wb_ref, wa_ref, rate_ref, bias_ref, normed_ref, scal_ref):
    tok = x_ref.shape[0]
    heads = wb_ref.shape[0]
    normed = rms_scale(x_ref[...].astype(F32), gain_ref[...]).astype(BF16)
    normed_ref[...] = normed
    beta = jax.nn.sigmoid(dot_nt(normed, wb_ref[...]))
    raw = dot_nt(normed, wa_ref[...]) + bias_ref[...]
    soft = jnp.maximum(raw, 0.0) + jnp.log1p(jnp.exp(-jnp.abs(raw)))
    log_decay = -rate_ref[...] * soft
    rows, cols = iotas(tok, tok)
    same = rows // BLOCK_LEN == cols // BLOCK_LEN
    run = jnp.dot((same & (rows >= cols)).astype(F32), log_decay, precision=HIGH, preferred_element_type=F32)
    full = jnp.dot(same.astype(F32), log_decay, precision=HIGH, preferred_element_type=F32)
    for place, value in enumerate((beta, run, jnp.exp(run), jnp.exp(full - run), jnp.exp(full))):
        scal_ref[:, place * heads : (place + 1) * heads] = value


def gate_kernel(meta_ref, normed_ref, w_gate_ref, x_ref, gate_ref, own_rows_ref, rows):
    tok = normed_ref.shape[0]
    depth = w_gate_ref.shape[0]
    lanes = own_rows_ref.shape[1]
    step = pl.program_id(0)

    @pl.when(step == 0)
    def _():
        gate_ref[...] = jnp.zeros_like(gate_ref)

    at = pl.multiple_of(step * depth, depth)
    gate_ref[...] += dot(normed_ref[:, pl.ds(at, depth)], w_gate_ref[...])

    @pl.when(step == pl.num_programs(0) - 1)
    def _():
        gate_ref[...] = jax.nn.silu(gate_ref[...])
        blocks = tok // BLOCK_LEN
        final = last_blocks(meta_ref)
        first = 0
        for ref in (gate_ref, x_ref):
            total = jnp.zeros((REQ, ref.shape[1]), F32)
            for block in range(blocks):
                end = (block + 1) * BLOCK_LEN
                line = ref[end - 8 : end, :].astype(F32)[7:8] if ref is gate_ref else ref[end - 16 : end, :].astype(F32)[15:16]
                total = total + jnp.where(final == meta_ref[REQ] * blocks + block, line, 0.0)
            for part in range(ref.shape[1] // lanes):
                rows[first : first + REQ, :] = total[:, part * lanes : (part + 1) * lanes]
                first += REQ
        own_rows_ref[...] = rows[...].astype(BF16)


def unit_lower_inverse(packed, spread, rows, cols):
    eye = (rows == cols).astype(F32)
    each = lambda fn, *lists: [fn(*items) for items in zip(*lists)]
    within = each(lambda m: jnp.where(rows // 8 == cols // 8, m, 0.0), packed)
    second = each(lambda m: dot3(m, spread(m)), within)
    fourth = each(lambda m: dot3(m, spread(m)), second)
    inverse = each(lambda m, n: dot3(eye - m, spread(eye + n)), within, second)
    inverse = each(lambda m, n: dot3(m, spread(eye + n)), inverse, fourth)
    width = 8
    while width < BLOCK_LEN:
        part = (rows // (2 * width) == cols // (2 * width)) & (rows // width != cols // width)
        left = each(lambda m, n: dot3(m, spread(jnp.where(part, n, 0.0))), inverse, packed)
        inverse = each(lambda m, n: m - dot3(n, spread(m)), inverse, left)
        width *= 2
    return inverse


def store_map(ref, at, a, b, eye):
    size = a.shape[0]
    diag = jnp.sum(jnp.where(eye, a, 0.0), axis=0, keepdims=True)
    high = diag.astype(BF16).astype(F32)
    low = diag - high
    place = lax.broadcasted_iota(jnp.int32, (PAD, size), 0)
    ref[at, :size, :] = jnp.where(eye, 0.0, a).astype(BF16)
    ref[at, size : size + PAD, :] = jnp.where(place == 0, high, jnp.where(place == 1, low, 0.0)).astype(BF16)
    ref[at, size + PAD : 2 * size + PAD, :] = b.astype(BF16)


def load_map(value, eye):
    size = value.shape[1]
    diag = value[size : size + PAD].astype(F32)
    a = value[:size].astype(F32) + jnp.where(eye, diag[0:1] + diag[1:2], 0.0)
    return a, value[size + PAD : 2 * size + PAD].astype(F32)


def maps_kernel(
    meta_ref, normed_ref, halo_ref, gain_hbm, wq_hbm, wk_hbm, wv_hbm, tq_hbm, tk_hbm, tv_hbm, scal_ref,
    maps_ref, qa_out, own_out, a_ref, b_ref, lhs, pre, qs, ks, vs, qa_ref, own_ref, a_buf, b_buf, sems,
    gain_ref, wq_ref, wk_ref, wv_ref, tq_ref, tk_ref, tv_ref, load_sems,
):
    loads = []
    for source, target in (
        (gain_hbm, gain_ref), (wq_hbm, wq_ref), (wk_hbm, wk_ref), (wv_hbm, wv_ref),
        (tq_hbm, tq_ref), (tk_hbm, tk_ref), (tv_hbm, tv_ref),
    ):
        loads.append(pltpu.make_async_copy(source, target, load_sems.at[len(loads)]))
        loads[-1].start()
    copies = []
    tok = normed_ref.shape[0]
    blocks = tok // BLOCK_LEN
    heads = qa_ref.shape[1]
    dk = qa_ref.shape[3]
    dv = own_ref.shape[3]
    rows_all = heads * BLOCK_LEN
    keep = []
    first_block = meta_ref[REQ] * blocks
    for block in range(blocks):
        offset = jnp.int32(0)
        flag = jnp.float32(1.0)
        for request in range(REQ):
            flag = jnp.where(offset == first_block + block, 0.0, flag)
            offset = offset + meta_ref[request]
        keep.append(flag)
    loads[0].wait()
    lhs[:HALO, :] = rms_scale(halo_ref[...].astype(F32), gain_ref[...]).astype(BF16)
    lhs[HALO:, :] = normed_ref[...]
    qk = heads * dk
    loads[1].wait()
    pre[:, :qk] = dot(lhs[...], wq_ref[...]).astype(BF16).astype(F32)
    loads[2].wait()
    pre[:, qk : 2 * qk] = dot(lhs[...], wk_ref[...]).astype(BF16).astype(F32)
    loads[3].wait()
    pre[:, 2 * qk :] = dot(lhs[...], wv_ref[...]).astype(BF16).astype(F32)
    for load in loads[4:]:
        load.wait()
    token = lax.broadcasted_iota(jnp.int32, (tok, 1), 0)
    masks = {}
    for lag in range(1, CONV):
        mask = jnp.ones((tok, 1), F32)
        for block in range(blocks):
            start = block * BLOCK_LEN
            mask = jnp.where((token >= start) & (token < start + lag), keep[block], mask)
        masks[lag] = mask

    def conv(first, taps_ref, at):
        total = None
        for tap in range(CONV):
            lag = CONV - 1 - tap
            part = pre[HALO - lag : HALO - lag + tok, first : first + dk] * taps_ref[tap : tap + 1, at : at + dk]
            if lag:
                part = part * masks[lag]
            total = part if total is None else total + part
        return jax.nn.silu(total)

    for head in range(heads):
        low = head * BLOCK_LEN
        for ref, base, taps_ref, scale in ((qs, 0, tq_ref, dk ** (-0.5)), (ks, qk, tk_ref, 1.0)):
            value = conv(base + head * dk, taps_ref, head * dk)
            value = value * (lax.rsqrt(jnp.sum(value * value, axis=-1, keepdims=True) + EPS) * scale)
            for block in range(blocks):
                ref[block, low : low + BLOCK_LEN, :] = value[block * BLOCK_LEN : (block + 1) * BLOCK_LEN]
        for part in range(dv // dk):
            at = head * dv + part * dk
            value = conv(2 * qk + at, tv_ref, at)
            for block in range(blocks):
                vs[block, low : low + BLOCK_LEN, part * dk : (part + 1) * dk] = value[
                    block * BLOCK_LEN : (block + 1) * BLOCK_LEN
                ]

    rows, cols = iotas(rows_all, rows_all)
    same = rows // BLOCK_LEN == cols // BLOCK_LEN
    p_rows, p_cols = iotas(BLOCK_LEN, rows_all)
    p_cols = p_cols % BLOCK_LEN
    spread = lambda value: jnp.where(same, jnp.concatenate([value] * heads, axis=0), 0.0)
    k_rows, k_cols = iotas(dk, dk)
    eye = k_rows == k_cols

    def column(place, block):
        span = slice(block * BLOCK_LEN, (block + 1) * BLOCK_LEN)
        at = place * heads
        return jnp.concatenate([scal_ref[span, at + head : at + head + 1] for head in range(heads)], axis=0)

    betas = [column(0, block) for block in range(blocks)]
    growths = [column(2, block) for block in range(blocks)]
    kbs = [ks[block].astype(BF16) for block in range(blocks)]
    p_head = lax.broadcasted_iota(jnp.int32, (BLOCK_LEN, rows_all), 1) // BLOCK_LEN
    p_lower = p_rows >= p_cols
    p_strict = p_rows > p_cols

    def choose(items):
        value = items[0]
        for head in range(1, heads):
            value = jnp.where(p_head == head, items[head], value)
        return value

    def pack(full):
        return choose([full[head * BLOCK_LEN : (head + 1) * BLOCK_LEN] for head in range(heads)])

    def beside(place, block):
        span = slice(block * BLOCK_LEN, (block + 1) * BLOCK_LEN)
        return choose([scal_ref[span, place * heads + head : place * heads + head + 1] for head in range(heads)])

    packed, scores = [], []
    for block in range(blocks):
        run = beside(1, block)
        across = jnp.sum(jnp.where(p_rows == p_cols, run, 0.0), axis=0, keepdims=True)
        decay = jnp.where(p_lower, jnp.exp(jnp.where(p_lower, run - across, 0.0)), 0.0)
        gram = pack(dot_nt(kbs[block], kbs[block]))
        packed.append(jnp.where(p_strict, beside(0, block) * gram * decay, 0.0))
        scores.append(spread(pack(dot_nt(qs[block].astype(BF16), kbs[block])) * decay).astype(BF16))
    inverses = unit_lower_inverse(packed, spread, p_rows, p_cols)
    wus = []
    for block in range(blocks):
        right = jnp.concatenate([(betas[block] * growths[block]) * ks[block], betas[block] * vs[block]], axis=1)
        wus.append(dot(spread(inverses[block]).astype(BF16), right.astype(BF16)).astype(BF16))
    q_effs, owns, tails = [], [], []
    for block in range(blocks):
        mixed = dot(scores[block], wus[block])
        q_effs.append((growths[block] * qs[block] - mixed[:, :dk]).astype(BF16))
        owns.append(mixed[:, dk:])
        tails.append((column(3, block) * ks[block]).astype(BF16))

    spans = [slice(head * BLOCK_LEN, (head + 1) * BLOCK_LEN) for head in range(heads)]
    joints = [None] * heads
    tail_place = lax.broadcasted_iota(jnp.int32, (PAD, dk), 0)
    for block in range(blocks):
        for head, span in enumerate(spans):
            grown = dot_tn(tails[block][span], wus[block][span])
            at = 4 * heads + head
            last = scal_ref[block * BLOCK_LEN : block * BLOCK_LEN + 1, at : at + 1]
            shrink, add = grown[:, :dk], grown[:, dk:]
            if block == 0:
                qa_ref[block, head] = (q_effs[block][span].astype(F32) * keep[0]).astype(BF16)
                own_ref[block, head] = owns[block][span]
                a_run = (jnp.where(eye, last, 0.0) - shrink) * keep[0]
                b_run = add
            else:
                joint = joints[head] * keep[block]
                joint_b = joint.astype(BF16)
                seen = dot(q_effs[block][span], joint_b)
                qa_ref[block, head] = seen[:, :dk].astype(BF16)
                own_ref[block, head] = seen[:, dk:] + owns[block][span]
                joint = last * joint - dot(shrink.astype(BF16), joint_b)
                a_run = joint[:, :dk]
                b_run = joint[:, dk:] + add
            joints[head] = jnp.concatenate([a_run, b_run], axis=1)
            a_buf[block, head] = a_run
            b_buf[block, head] = b_run
            if block == blocks - 1:
                for part in range(2):
                    to = 2 * head + part
                    store_map(maps_ref, to, a_run, b_run[:, part * dk : (part + 1) * dk], eye)
                    lines = []
                    for row in range(blocks):
                        lines.append(qa_ref[row, head, BLOCK_LEN - 1 :, :].astype(F32))
                    for row in range(blocks):
                        lines.append(own_ref[row, head, BLOCK_LEN - 1 :, part * dk : (part + 1) * dk])
                    tail_rows = jnp.zeros((PAD, dk), F32)
                    for row, line in enumerate(lines):
                        tail_rows = jnp.where(tail_place == row, line, tail_rows)
                    maps_ref[to, 2 * dk + PAD :, :] = tail_rows.astype(BF16)
        for place, (buf, ref) in enumerate(
            ((qa_ref, qa_out), (own_ref, own_out), (a_buf, a_ref), (b_buf, b_ref))
        ):
            copies.append(pltpu.make_async_copy(buf.at[block], ref.at[block], sems.at[place, block]))
            copies[-1].start()
    for copy in copies:
        copy.wait()


def scan_kernel(got_ref, before_ref, total_ref):
    size = got_ref.shape[2]
    rows, cols = iotas(size, size)
    eye = rows == cols
    run = None
    for member in range(GROUP):
        a, b = load_map(got_ref[member], eye)
        if run is None:
            before_ref[member] = jnp.concatenate([eye.astype(F32), jnp.zeros((size, size), F32)], axis=1)
            run = jnp.concatenate([a, b], axis=1)
        else:
            before_ref[member] = run
            run = dot3(a, run)
            run = jnp.concatenate([run[:, :size], run[:, size:] + b], axis=1)
    store_map(total_ref, 0, run[:, :size], run[:, size:], eye)


def apply_kernel(meta_ref, one_ref, two_ref, before_ref, got_ref, gain_ref, own_rows_ref, out_ref, tail):
    size = one_ref.shape[2]
    blocks = PAD // 4
    rows, cols = iotas(size, size)
    eye = rows == cols
    a, b = load_map(one_ref[0], eye)
    a_high, a_low = split(a)
    entering = dot(a_high, two_ref[...]) + dot(a_low, two_ref[...]) + b
    e_high, e_low = split(entering)
    part = meta_ref[REQ] % 2
    group = meta_ref[REQ] // GROUP
    gain = jnp.where(part == 0, gain_ref[:, :size], gain_ref[:, size:])
    final = last_blocks(meta_ref)
    kept = [jnp.zeros((REQ, size), F32), jnp.zeros((REQ, 1), F32)]
    for member in range(GROUP):
        p_high, p_low = split(before_ref[member, :, :size])
        value = dot(p_high, e_high) + dot(p_high, e_low) + dot(p_low, e_high) + before_ref[member, :, size:]
        state = value.astype(BF16)
        out_ref[member, :size, :] = state
        extra = got_ref[member, 2 * size + PAD :, :]
        out = dot(extra, state)[:blocks] + extra.astype(F32)[blocks : 2 * blocks]
        squares = jnp.sum(out * out, axis=1, keepdims=True)
        gained = out * gain
        for block in range(blocks):
            hit = final == (group * GROUP + member) * blocks + block
            for index, line in enumerate((gained[block : block + 1], squares[block : block + 1])):
                kept[index] = kept[index] + jnp.where(hit, line, 0.0)
    lane = lax.broadcasted_iota(jnp.int32, (REQ, size), 1)
    high = kept[1].astype(BF16).astype(F32)
    tail[...] = jnp.zeros_like(tail)
    tail[:REQ, :] = kept[0]
    tail[REQ : 2 * REQ, :] = jnp.where(lane == 0, high, jnp.where(lane == 1, kept[1] - high, 0.0))
    own = own_rows_ref.shape[0]
    for member in range(GROUP):
        out_ref[member, size : size + own, :] = own_rows_ref[...]
        out_ref[member, size + own :, :] = tail[...].astype(BF16)


def output_kernel(s_ref, qa_ref, own_ref, gate_ref, gain_ref, gated_ref):
    blocks, heads, block_len, dk = qa_ref.shape
    tok = blocks * block_len
    dv = own_ref.shape[3]
    for head in range(heads):
        state = jnp.concatenate([s_ref[2 * head], s_ref[2 * head + 1]], axis=1)
        out = dot(qa_ref[:, head].reshape(tok, dk), state) + own_ref[:, head].reshape(tok, dv)
        span = slice(head * dv, (head + 1) * dv)
        gated_ref[:, span] = (rms_scale(out, gain_ref[...]) * gate_ref[:, span]).astype(BF16)


def mix_kernel(meta_ref, gated_ref, w_ref, x_ref, one_ref, two_ref, three_ref, here_ref):
    step = pl.program_id(0)
    value = dot(gated_ref[...], w_ref[...])
    for place, ref in enumerate((one_ref, two_ref, three_ref)):

        @pl.when(step == place)
        def _():
            ref[...] = value.astype(BF16)

    @pl.when(step == pl.num_programs(0) - 1)
    def _():
        here_ref[...] = value + x_ref[...].astype(F32)


def rows_kernel(meta_ref, rows_ref, w_ref, send_ref, gated, sums, lines):
    step = pl.program_id(0)
    heads = pl.num_programs(0)
    dk = rows_ref.shape[2]
    share = w_ref.shape[1] // 4
    own = rows_ref.shape[1] - PAD

    @pl.when(step == 0)
    def _():
        total = rows_ref[0, :own].astype(F32)
        for member in range(1, GROUP):
            total = total + rows_ref[member, :own].astype(F32)
        lines[...] = total
        tails = [rows_ref[member, own:].astype(F32) for member in range(GROUP)]
        for head in range(heads):
            both = tails[2 * head][REQ : 2 * REQ] + tails[2 * head + 1][REQ : 2 * REQ]
            scale = lax.rsqrt(jnp.sum(both, axis=1, keepdims=True) / (2 * dk) + EPS)
            for part in range(2):
                member = 2 * head + part
                value = tails[member][:REQ] * scale * lines[member * REQ : (member + 1) * REQ, :]
                gated[head, :, part * dk : (part + 1) * dk] = value.astype(BF16)
        sums[...] = jnp.zeros_like(sums)
        for place in range(share // dk):
            at = pl.multiple_of(meta_ref[REQ + 1] * share + place * dk, dk)
            first = (GROUP + place) * REQ
            sums[:, pl.ds(at, dk)] = lines[first : first + REQ, :]

    sums[...] += dot(gated[step], w_ref[...])

    @pl.when(step == heads - 1)
    def _():
        value = sums[...].astype(BF16)
        for target in range(send_ref.shape[0]):
            send_ref[target] = value


def head_kernel(lasts_ref, gain_ref, w_ref, out_ref):
    last = jnp.sum(lasts_ref[...].astype(F32), axis=0).astype(BF16).astype(F32)
    final = rms_scale(last, gain_ref[...]).astype(BF16)
    best = jnp.max(dot(final, w_ref[...]), axis=1, keepdims=True)
    place, lane = iotas(best.shape[0], out_ref.shape[2])
    row = jnp.sum(jnp.where(place == lane, best, 0.0), axis=0, keepdims=True)
    out_ref[...] = jnp.broadcast_to(row[None], out_ref.shape)


def states_kernel(a_ref, b_ref, s_ref, out_ref):
    heads = a_ref.shape[1]
    for head in range(heads):
        state = jnp.concatenate([s_ref[2 * head], s_ref[2 * head + 1]], axis=1)
        high, low = split(a_ref[0, head])
        out_ref[0, head] = dot(high, state) + dot(low, state) + b_ref[0, head]


REQ = 4


def body(
    states_in, lengths, attn_gain, w_query, w_key, w_value, w_gate, w_beta, w_alpha, decay_rate,
    decay_bias, conv_query, conv_key, conv_value, out_gain, w_out, final_gain, w_head,
):
    tok, model = states_in.shape
    heads = decay_rate.shape[0]
    dk = w_query.shape[1] // heads
    dv = w_value.shape[1] // heads
    blocks = tok // BLOCK_LEN
    seq_count = lax.axis_size("seq")
    tp_count = lax.axis_size("tp")
    piece = lax.axis_index("seq")
    shard = lax.axis_index("tp")
    share = model // tp_count
    rows_all = heads * BLOCK_LEN
    shape = jax.ShapeDtypeStruct
    params = lambda mib: pltpu.CompilerParams(vmem_limit_bytes=mib << 20)
    meta = jnp.concatenate([lengths, piece[None], shard[None]]).astype(jnp.int32)

    halo = lax.ppermute(states_in[tok - HALO :], "seq", [(i, i + 1) for i in range(seq_count - 1)])
    gain = attn_gain[None, :]
    normed, scal = pl.pallas_call(
        norm_kernel,
        out_shape=(shape((tok, model), BF16), shape((tok, 128), F32)),
        grid=(1,),
        in_specs=[
            whole(tok, model), whole(1, model), whole(heads, model), whole(heads, model), whole(1, heads),
            whole(1, heads),
        ],
        out_specs=(whole(tok, model), whole(tok, 128)),
        compiler_params=params(24),
        name="norm_kernel",
    )(*hbm(states_in, gain, w_beta.T, w_alpha.T, decay_rate[None, :], decay_bias[None, :]))

    maps, qa, own, a_all, b_all = pl.pallas_call(
        maps_kernel,
        out_shape=(
            shape((2 * heads, 2 * dk + 2 * PAD, dk), BF16),
            pltpu.HBM((blocks, heads, BLOCK_LEN, dk), BF16),
            pltpu.HBM((blocks, heads, BLOCK_LEN, dv), F32),
            pltpu.HBM((blocks, heads, dk, dk), F32),
            pltpu.HBM((blocks, heads, dk, dv), F32),
        ),
        in_specs=[SMEM, VMEM, VMEM] + [HBM] * 7 + [VMEM],
        out_specs=(VMEM, HBM, HBM, HBM, HBM),
        scratch_shapes=[
            pltpu.VMEM((HALO + tok, model), BF16),
            pltpu.VMEM((HALO + tok, 2 * heads * dk + heads * dv), F32),
            pltpu.VMEM((blocks, rows_all, dk), F32),
            pltpu.VMEM((blocks, rows_all, dk), F32),
            pltpu.VMEM((blocks, rows_all, dv), F32),
            pltpu.VMEM((blocks, heads, BLOCK_LEN, dk), BF16),
            pltpu.VMEM((blocks, heads, BLOCK_LEN, dv), F32),
            pltpu.VMEM((blocks, heads, dk, dk), F32),
            pltpu.VMEM((blocks, heads, dk, dv), F32),
            pltpu.SemaphoreType.DMA((4, blocks)),
            pltpu.VMEM((1, model), F32),
            pltpu.VMEM(w_query.shape, BF16),
            pltpu.VMEM(w_key.shape, BF16),
            pltpu.VMEM(w_value.shape, BF16),
            pltpu.VMEM(conv_query.shape, F32),
            pltpu.VMEM(conv_key.shape, F32),
            pltpu.VMEM(conv_value.shape, F32),
            pltpu.SemaphoreType.DMA((7,)),
        ],
        compiler_params=params(40),
        name="maps_kernel",
    )(meta, normed, halo, *hbm(gain, w_query, w_key, w_value, conv_query, conv_key, conv_value), scal)

    got = group_exchange(maps)
    gate, own_rows = pl.pallas_call(
        gate_kernel,
        out_shape=(shape((tok, heads * dv), F32), shape((REQ * 3 * heads, dk), BF16)),
        grid_spec=pltpu.PrefetchScalarGridSpec(
            num_scalar_prefetch=1,
            grid=(heads,),
            in_specs=[
                whole(tok, model),
                pl.BlockSpec((model // heads, heads * dv), lambda i, m: (i, 0)),
                pl.BlockSpec((tok, share), lambda i, m: (0, m[REQ + 1])),
            ],
            out_specs=(whole(tok, heads * dv), whole(REQ * 3 * heads, dk)),
            scratch_shapes=[pltpu.VMEM((REQ * 3 * heads, dk), F32)],
        ),
        compiler_params=params(24),
        name="gate_kernel",
    )(meta, *hbm(normed, w_gate, states_in))
    got, gate, own_rows = lax.optimization_barrier((got, gate, own_rows))
    before, total = pl.pallas_call(
        scan_kernel,
        out_shape=(shape((GROUP, dk, 2 * dk), F32), shape((1, 2 * dk + PAD, dk), BF16)),
        in_specs=[VMEM],
        out_specs=(VMEM,) * 2,
        compiler_params=params(16),
        name="scan_kernel",
    )(got)
    one_back = shift_groups(total, 1)
    two_back = shift_groups(total[0, dk + PAD :], 2)
    rows_len = own_rows.shape[0] + PAD
    incoming = pl.pallas_call(
        apply_kernel,
        out_shape=shape((GROUP, dk + rows_len, dk), BF16),
        in_specs=[SMEM] + [VMEM] * 6,
        out_specs=VMEM,
        scratch_shapes=[pltpu.VMEM((PAD, dk), F32)],
        compiler_params=params(16),
        name="apply_kernel",
    )(meta, one_back, two_back, before, got, out_gain[None, :], own_rows)
    s_in = group_exchange(incoming)

    groups = seq_count // GROUP
    joint = [
        [(GROUP * group + member) * tp_count + column for group in range(groups) for column in range(tp_count)]
        for member in range(GROUP)
    ]
    sends = pl.pallas_call(
        rows_kernel,
        out_shape=shape((groups * tp_count, REQ, model), BF16),
        grid_spec=pltpu.PrefetchScalarGridSpec(
            num_scalar_prefetch=1,
            grid=(heads,),
            in_specs=[
                pl.BlockSpec((GROUP, rows_len, dk), lambda i, m: (0, dk // rows_len, 0)),
                pl.BlockSpec((dv, model), lambda i, m: (i, 0)),
            ],
            out_specs=whole(groups * tp_count, REQ, model),
            scratch_shapes=[
                pltpu.VMEM((heads, REQ, dv), BF16),
                pltpu.VMEM((REQ, model), F32),
                pltpu.VMEM((rows_len - PAD, dk), F32),
            ],
        ),
        compiler_params=params(24),
        name="rows_kernel",
    )(meta, *hbm(s_in, w_out))
    sends, s_after = lax.optimization_barrier((sends, s_in))
    lasts = lax.all_to_all(sends, ("seq", "tp"), 0, 0, axis_index_groups=joint)
    gated = pl.pallas_call(
        output_kernel,
        out_shape=shape((tok, heads * dv), BF16),
        grid=(1,),
        in_specs=[
            whole(2 * heads, dk, dk),
            whole(blocks, heads, BLOCK_LEN, dk),
            whole(blocks, heads, BLOCK_LEN, dv),
            whole(tok, heads * dv),
            whole(1, dv),
        ],
        out_specs=whole(tok, heads * dv),
        compiler_params=params(24),
        name="output_kernel",
    )(s_after, qa, own, gate, out_gain[None, :])

    turn = lambda i, m: (m[REQ + 1] + i + 1) % tp_count
    one, two, three, here = pl.pallas_call(
        mix_kernel,
        out_shape=(shape((tok, share), BF16),) * 3 + (shape((tok, share), F32),),
        grid_spec=pltpu.PrefetchScalarGridSpec(
            num_scalar_prefetch=1,
            grid=(tp_count,),
            in_specs=[
                whole(tok, heads * dv),
                pl.BlockSpec((heads * dv, share), lambda i, m: (0, turn(i, m))),
                pl.BlockSpec((tok, share), lambda i, m: (0, m[REQ + 1])),
            ],
            out_specs=(whole(tok, share),) * 4,
        ),
        compiler_params=params(24),
        name="mix_kernel",
    )(meta, gated, *hbm(w_out, states_in))

    rings = [[(i, (i + offset) % tp_count) for i in range(tp_count)] for offset in range(1, tp_count)]
    spread = pl.pallas_call(
        head_kernel,
        out_shape=shape((seq_count * tp_count, 1, 128), F32),
        grid=(1,),
        in_specs=[whole(groups * tp_count, REQ, model), whole(1, model), whole(*w_head.shape)],
        out_specs=whole(seq_count * tp_count, 1, 128),
        compiler_params=params(24),
        name="head_kernel",
    )(lasts, final_gain[None, :], w_head)
    spread, s_late = lax.optimization_barrier((spread, s_after))
    bests = lax.all_to_all(spread, ("seq", "tp"), 0, 0)
    block_states = pl.pallas_call(
        states_kernel,
        out_shape=shape((blocks, heads, dk, dv), F32),
        grid=(blocks,),
        in_specs=[
            pl.BlockSpec((1, heads, dk, dk), lambda i: (i, 0, 0, 0)),
            pl.BlockSpec((1, heads, dk, dv), lambda i: (i, 0, 0, 0)),
            pl.BlockSpec((2 * heads, dk, dk), lambda i: (0, 0, 0)),
        ],
        out_specs=pl.BlockSpec((1, heads, dk, dv), lambda i: (i, 0, 0, 0)),
        compiler_params=params(16),
        name="states_kernel",
    )(*hbm(a_all, b_all, s_late))

    mixed = here
    for ring, value in zip(rings, (one, two, three)):
        mixed = mixed + lax.ppermute(value, "tp", ring).astype(F32)
    hidden = mixed.astype(BF16)
    max_logit = jnp.max(bests[:, 0, :REQ], axis=0)
    return (hidden, block_states, max_logit)


def solution(mesh):
    return jax.shard_map(
        body,
        mesh=mesh,
        in_specs=(
            P("seq", None), P(), P(), P(None, "tp"), P(None, "tp"), P(None, "tp"), P(None, "tp"),
            P(None, "tp"), P(None, "tp"), P("tp"), P("tp"), P(None, "tp"), P(None, "tp"), P(None, "tp"),
            P(), P("tp", None), P(), P(None, ("seq", "tp")),
        ),
        out_specs=(P("seq", "tp"), P("seq", "tp", None, None), P()),
        check_vma=False,
    )
```

```python
import jax
import jax.numpy as jnp
from jax import lax
from jax.experimental import pallas as pl
from jax.experimental.pallas import tpu as pltpu
from jax.sharding import PartitionSpec as P


CONV = 4
BLOCK_LEN = 64
GROUP = 8
HALO = 16
PAD = 16
EPS = 1e-06
HIGH = lax.Precision.HIGHEST
F32 = jnp.float32
BF16 = jnp.bfloat16

VMEM = pl.BlockSpec(memory_space=pltpu.VMEM)
HBM = pl.BlockSpec(memory_space=pltpu.HBM)
SMEM = pl.BlockSpec(memory_space=pltpu.SMEM)


def whole(*dims):
    return pl.BlockSpec(dims, lambda *_: (0,) * len(dims))


def hbm(*values):
    return [pltpu.with_memory_space_constraint(value, pltpu.HBM) for value in values]


def rms_scale(values, gain):
    return values * lax.rsqrt(jnp.mean(values * values, axis=-1, keepdims=True) + EPS) * gain


def shift_groups(value, steps):
    count = lax.axis_size("seq")
    gap = steps * GROUP
    return lax.ppermute(value, "seq", [(source, source + gap) for source in range(count - gap)])


def group_exchange(value):
    count = lax.axis_size("seq")
    groups = [list(range(first, first + GROUP)) for first in range(0, count, GROUP)]
    return lax.all_to_all(value, "seq", 0, 0, axis_index_groups=groups)


def dot(a, b):
    return jnp.dot(a, b, preferred_element_type=F32)


def dot_nt(a, b):
    return lax.dot_general(a, b, (((1,), (1,)), ((), ())), preferred_element_type=F32)


def dot_tn(a, b):
    return lax.dot_general(a, b, (((0,), (0,)), ((), ())), preferred_element_type=F32)


def split(a):
    high = a.astype(BF16)
    return high, (a - high.astype(F32)).astype(BF16)


def dot3(a, b):
    a_high, a_low = split(a)
    b_high, b_low = split(b)
    return dot(a_high, b_high) + dot(a_high, b_low) + dot(a_low, b_high)


def iotas(rows, cols):
    return (
        lax.broadcasted_iota(jnp.int32, (rows, cols), 0),
        lax.broadcasted_iota(jnp.int32, (rows, cols), 1),
    )


def last_blocks(meta_ref):
    place = lax.broadcasted_iota(jnp.int32, (REQ, 1), 0)
    final = jnp.zeros((REQ, 1), jnp.int32)
    end = jnp.int32(0)
    for request in range(REQ):
        end = end + meta_ref[request]
        final = jnp.where(place == request, end - 1, final)
    return final


def fill_scalars(normed, wb_ref, wa_ref, rate_ref, bias_ref, scal_ref):
    tok = normed.shape[0]
    heads = wb_ref.shape[0]
    beta = jax.nn.sigmoid(dot_nt(normed, wb_ref[...]))
    raw = dot_nt(normed, wa_ref[...]) + bias_ref[...]
    soft = jnp.maximum(raw, 0.0) + jnp.log1p(jnp.exp(-jnp.abs(raw)))
    log_decay = -rate_ref[...] * soft
    rows, cols = iotas(tok, tok)
    same = rows // BLOCK_LEN == cols // BLOCK_LEN
    run = jnp.dot((same & (rows >= cols)).astype(F32), log_decay, precision=HIGH, preferred_element_type=F32)
    full = jnp.dot(same.astype(F32), log_decay, precision=HIGH, preferred_element_type=F32)
    for place, value in enumerate((beta, run, jnp.exp(run), jnp.exp(full - run), jnp.exp(full))):
        scal_ref[:, place * heads : (place + 1) * heads] = value


def gate_kernel(meta_ref, normed_ref, w_gate_ref, x_ref, gate_ref, own_rows_ref, rows):
    tok = normed_ref.shape[0]
    depth = w_gate_ref.shape[0]
    lanes = own_rows_ref.shape[1]
    step = pl.program_id(0)

    @pl.when(step == 0)
    def _():
        gate_ref[...] = jnp.zeros_like(gate_ref)

    at = pl.multiple_of(step * depth, depth)
    gate_ref[...] += dot(normed_ref[:, pl.ds(at, depth)], w_gate_ref[...])

    @pl.when(step == pl.num_programs(0) - 1)
    def _():
        gate_ref[...] = jax.nn.silu(gate_ref[...])
        blocks = tok // BLOCK_LEN
        final = last_blocks(meta_ref)
        first = 0
        for ref in (gate_ref, x_ref):
            total = jnp.zeros((REQ, ref.shape[1]), F32)
            for block in range(blocks):
                end = (block + 1) * BLOCK_LEN
                line = ref[end - 8 : end, :].astype(F32)[7:8] if ref is gate_ref else ref[end - 16 : end, :].astype(F32)[15:16]
                total = total + jnp.where(final == meta_ref[REQ] * blocks + block, line, 0.0)
            for part in range(ref.shape[1] // lanes):
                rows[first : first + REQ, :] = total[:, part * lanes : (part + 1) * lanes]
                first += REQ
        own_rows_ref[...] = rows[...].astype(BF16)


def unit_lower_inverse(packed, spread, rows, cols):
    eye = (rows == cols).astype(F32)
    each = lambda fn, *lists: [fn(*items) for items in zip(*lists)]
    within = each(lambda m: jnp.where(rows // 8 == cols // 8, m, 0.0), packed)
    second = each(lambda m: dot3(m, spread(m)), within)
    fourth = each(lambda m: dot3(m, spread(m)), second)
    inverse = each(lambda m, n: dot3(eye - m, spread(eye + n)), within, second)
    inverse = each(lambda m, n: dot3(m, spread(eye + n)), inverse, fourth)
    width = 8
    while width < BLOCK_LEN:
        part = (rows // (2 * width) == cols // (2 * width)) & (rows // width != cols // width)
        left = each(lambda m, n: dot3(m, spread(jnp.where(part, n, 0.0))), inverse, packed)
        inverse = each(lambda m, n: m - dot3(n, spread(m)), inverse, left)
        width *= 2
    return inverse


def store_map(ref, at, a, b, eye):
    size = a.shape[0]
    diag = jnp.sum(jnp.where(eye, a, 0.0), axis=0, keepdims=True)
    high = diag.astype(BF16).astype(F32)
    low = diag - high
    place = lax.broadcasted_iota(jnp.int32, (PAD, size), 0)
    ref[at, :size, :] = jnp.where(eye, 0.0, a).astype(BF16)
    ref[at, size : size + PAD, :] = jnp.where(place == 0, high, jnp.where(place == 1, low, 0.0)).astype(BF16)
    ref[at, size + PAD : 2 * size + PAD, :] = b.astype(BF16)


def load_map(value, eye):
    size = value.shape[1]
    diag = value[size : size + PAD].astype(F32)
    a = value[:size].astype(F32) + jnp.where(eye, diag[0:1] + diag[1:2], 0.0)
    return a, value[size + PAD : 2 * size + PAD].astype(F32)


def maps_kernel(
    meta_ref, halo_ref, x_hbm, gain_hbm, wb_hbm, wa_hbm, rate_hbm, bias_hbm, wq_hbm, wk_hbm, wv_hbm,
    tq_hbm, tk_hbm, tv_hbm,
    maps_ref, normed_out, qa_out, own_out, a_ref, b_ref, lhs, pre, qs, ks, vs, qa_ref, own_ref, a_buf, b_buf, sems,
    scal_ref, x_ref, gain_ref, wb_ref, wa_ref, rate_ref, bias_ref, wq_ref, wk_ref, wv_ref,
    tq_ref, tk_ref, tv_ref, load_sems, normed_sem,
):
    loads = []
    for source, target in (
        (x_hbm, x_ref), (gain_hbm, gain_ref), (wq_hbm, wq_ref), (wk_hbm, wk_ref), (wb_hbm, wb_ref),
        (wa_hbm, wa_ref), (rate_hbm, rate_ref), (bias_hbm, bias_ref), (tq_hbm, tq_ref), (tk_hbm, tk_ref),
        (wv_hbm, wv_ref), (tv_hbm, tv_ref),
    ):
        loads.append(pltpu.make_async_copy(source, target, load_sems.at[len(loads)]))
        loads[-1].start()
    copies = []
    tok = x_ref.shape[0]
    blocks = tok // BLOCK_LEN
    heads = qa_ref.shape[1]
    dk = qa_ref.shape[3]
    dv = own_ref.shape[3]
    rows_all = heads * BLOCK_LEN
    keep = []
    first_block = meta_ref[REQ] * blocks
    for block in range(blocks):
        offset = jnp.int32(0)
        flag = jnp.float32(1.0)
        for request in range(REQ):
            flag = jnp.where(offset == first_block + block, 0.0, flag)
            offset = offset + meta_ref[request]
        keep.append(flag)
    loads[0].wait()
    loads[1].wait()
    lhs[:HALO, :] = rms_scale(halo_ref[...].astype(F32), gain_ref[...]).astype(BF16)
    lhs[HALO:, :] = rms_scale(x_ref[...].astype(F32), gain_ref[...]).astype(BF16)
    copies.append(pltpu.make_async_copy(lhs.at[pl.ds(HALO, tok), :], normed_out, normed_sem.at[0]))
    copies[-1].start()
    qk = heads * dk
    loads[2].wait()
    pre[:, :qk] = dot(lhs[...], wq_ref[...]).astype(BF16).astype(F32)
    for load in loads[3:10]:
        load.wait()
    pre[:, qk : 2 * qk] = dot(lhs[...], wk_ref[...]).astype(BF16).astype(F32)
    fill_scalars(lhs[HALO:, :], wb_ref, wa_ref, rate_ref, bias_ref, scal_ref)
    token = lax.broadcasted_iota(jnp.int32, (tok, 1), 0)
    masks = {}
    for lag in range(1, CONV):
        mask = jnp.ones((tok, 1), F32)
        for block in range(blocks):
            start = block * BLOCK_LEN
            mask = jnp.where((token >= start) & (token < start + lag), keep[block], mask)
        masks[lag] = mask

    def conv(first, taps_ref, at):
        total = None
        for tap in range(CONV):
            lag = CONV - 1 - tap
            part = pre[HALO - lag : HALO - lag + tok, first : first + dk] * taps_ref[tap : tap + 1, at : at + dk]
            if lag:
                part = part * masks[lag]
            total = part if total is None else total + part
        return jax.nn.silu(total)

    for head in range(heads):
        low = head * BLOCK_LEN
        for ref, base, taps_ref, scale in ((qs, 0, tq_ref, dk ** (-0.5)), (ks, qk, tk_ref, 1.0)):
            value = conv(base + head * dk, taps_ref, head * dk)
            value = value * (lax.rsqrt(jnp.sum(value * value, axis=-1, keepdims=True) + EPS) * scale)
            for block in range(blocks):
                ref[block, low : low + BLOCK_LEN, :] = value[block * BLOCK_LEN : (block + 1) * BLOCK_LEN]
    for load in loads[10:]:
        load.wait()
    pre[:, 2 * qk :] = dot(lhs[...], wv_ref[...]).astype(BF16).astype(F32)
    for head in range(heads):
        low = head * BLOCK_LEN
        for part in range(dv // dk):
            at = head * dv + part * dk
            value = conv(2 * qk + at, tv_ref, at)
            for block in range(blocks):
                vs[block, low : low + BLOCK_LEN, part * dk : (part + 1) * dk] = value[
                    block * BLOCK_LEN : (block + 1) * BLOCK_LEN
                ]

    rows, cols = iotas(rows_all, rows_all)
    same = rows // BLOCK_LEN == cols // BLOCK_LEN
    p_rows, p_cols = iotas(BLOCK_LEN, rows_all)
    p_cols = p_cols % BLOCK_LEN
    spread = lambda value: jnp.where(same, jnp.concatenate([value] * heads, axis=0), 0.0)
    k_rows, k_cols = iotas(dk, dk)
    eye = k_rows == k_cols

    def column(place, block):
        span = slice(block * BLOCK_LEN, (block + 1) * BLOCK_LEN)
        at = place * heads
        return jnp.concatenate([scal_ref[span, at + head : at + head + 1] for head in range(heads)], axis=0)

    betas = [column(0, block) for block in range(blocks)]
    growths = [column(2, block) for block in range(blocks)]
    kbs = [ks[block].astype(BF16) for block in range(blocks)]
    p_head = lax.broadcasted_iota(jnp.int32, (BLOCK_LEN, rows_all), 1) // BLOCK_LEN
    p_lower = p_rows >= p_cols
    p_strict = p_rows > p_cols

    def choose(items):
        value = items[0]
        for head in range(1, heads):
            value = jnp.where(p_head == head, items[head], value)
        return value

    def pack(full):
        return choose([full[head * BLOCK_LEN : (head + 1) * BLOCK_LEN] for head in range(heads)])

    def beside(place, block):
        span = slice(block * BLOCK_LEN, (block + 1) * BLOCK_LEN)
        return choose([scal_ref[span, place * heads + head : place * heads + head + 1] for head in range(heads)])

    packed, scores = [], []
    for block in range(blocks):
        run = beside(1, block)
        across = jnp.sum(jnp.where(p_rows == p_cols, run, 0.0), axis=0, keepdims=True)
        decay = jnp.where(p_lower, jnp.exp(jnp.where(p_lower, run - across, 0.0)), 0.0)
        gram = pack(dot_nt(kbs[block], kbs[block]))
        packed.append(jnp.where(p_strict, beside(0, block) * gram * decay, 0.0))
        scores.append(spread(pack(dot_nt(qs[block].astype(BF16), kbs[block])) * decay).astype(BF16))
    inverses = unit_lower_inverse(packed, spread, p_rows, p_cols)
    wus = []
    for block in range(blocks):
        right = jnp.concatenate([(betas[block] * growths[block]) * ks[block], betas[block] * vs[block]], axis=1)
        wus.append(dot(spread(inverses[block]).astype(BF16), right.astype(BF16)).astype(BF16))
    q_effs, owns, tails = [], [], []
    for block in range(blocks):
        mixed = dot(scores[block], wus[block])
        q_effs.append((growths[block] * qs[block] - mixed[:, :dk]).astype(BF16))
        owns.append(mixed[:, dk:])
        tails.append((column(3, block) * ks[block]).astype(BF16))

    spans = [slice(head * BLOCK_LEN, (head + 1) * BLOCK_LEN) for head in range(heads)]
    joints = [None] * heads
    tail_place = lax.broadcasted_iota(jnp.int32, (PAD, dk), 0)
    for block in range(blocks):
        for head, span in enumerate(spans):
            grown = dot_tn(tails[block][span], wus[block][span])
            at = 4 * heads + head
            last = scal_ref[block * BLOCK_LEN : block * BLOCK_LEN + 1, at : at + 1]
            shrink, add = grown[:, :dk], grown[:, dk:]
            if block == 0:
                qa_ref[block, head] = (q_effs[block][span].astype(F32) * keep[0]).astype(BF16)
                own_ref[block, head] = owns[block][span]
                a_run = (jnp.where(eye, last, 0.0) - shrink) * keep[0]
                b_run = add
            else:
                joint = joints[head] * keep[block]
                joint_b = joint.astype(BF16)
                seen = dot(q_effs[block][span], joint_b)
                qa_ref[block, head] = seen[:, :dk].astype(BF16)
                own_ref[block, head] = seen[:, dk:] + owns[block][span]
                joint = last * joint - dot(shrink.astype(BF16), joint_b)
                a_run = joint[:, :dk]
                b_run = joint[:, dk:] + add
            joints[head] = jnp.concatenate([a_run, b_run], axis=1)
            a_buf[block, head] = a_run
            b_buf[block, head] = b_run
            if block == blocks - 1:
                for part in range(2):
                    to = 2 * head + part
                    store_map(maps_ref, to, a_run, b_run[:, part * dk : (part + 1) * dk], eye)
                    lines = []
                    for row in range(blocks):
                        lines.append(qa_ref[row, head, BLOCK_LEN - 1 :, :].astype(F32))
                    for row in range(blocks):
                        lines.append(own_ref[row, head, BLOCK_LEN - 1 :, part * dk : (part + 1) * dk])
                    tail_rows = jnp.zeros((PAD, dk), F32)
                    for row, line in enumerate(lines):
                        tail_rows = jnp.where(tail_place == row, line, tail_rows)
                    maps_ref[to, 2 * dk + PAD :, :] = tail_rows.astype(BF16)
        for place, (buf, ref) in enumerate(
            ((qa_ref, qa_out), (own_ref, own_out), (a_buf, a_ref), (b_buf, b_ref))
        ):
            copies.append(pltpu.make_async_copy(buf.at[block], ref.at[block], sems.at[place, block]))
            copies[-1].start()
    for copy in copies:
        copy.wait()


def scan_kernel(got_ref, before_ref, total_ref):
    size = got_ref.shape[2]
    rows, cols = iotas(size, size)
    eye = rows == cols
    run = None
    for member in range(GROUP):
        a, b = load_map(got_ref[member], eye)
        if run is None:
            before_ref[member] = jnp.concatenate([eye.astype(F32), jnp.zeros((size, size), F32)], axis=1)
            run = jnp.concatenate([a, b], axis=1)
        else:
            before_ref[member] = run
            run = dot3(a, run)
            run = jnp.concatenate([run[:, :size], run[:, size:] + b], axis=1)
    store_map(total_ref, 0, run[:, :size], run[:, size:], eye)


def apply_kernel(meta_ref, one_ref, two_ref, before_ref, got_ref, gain_ref, own_rows_ref, out_ref, tail):
    size = one_ref.shape[2]
    blocks = PAD // 4
    rows, cols = iotas(size, size)
    eye = rows == cols
    a, b = load_map(one_ref[0], eye)
    a_high, a_low = split(a)
    entering = dot(a_high, two_ref[...]) + dot(a_low, two_ref[...]) + b
    e_high, e_low = split(entering)
    part = meta_ref[REQ] % 2
    group = meta_ref[REQ] // GROUP
    gain = jnp.where(part == 0, gain_ref[:, :size], gain_ref[:, size:])
    final = last_blocks(meta_ref)
    kept = [jnp.zeros((REQ, size), F32), jnp.zeros((REQ, 1), F32)]
    for member in range(GROUP):
        p_high, p_low = split(before_ref[member, :, :size])
        value = dot(p_high, e_high) + dot(p_high, e_low) + dot(p_low, e_high) + before_ref[member, :, size:]
        state = value.astype(BF16)
        out_ref[member, :size, :] = state
        extra = got_ref[member, 2 * size + PAD :, :]
        out = dot(extra, state)[:blocks] + extra.astype(F32)[blocks : 2 * blocks]
        squares = jnp.sum(out * out, axis=1, keepdims=True)
        gained = out * gain
        for block in range(blocks):
            hit = final == (group * GROUP + member) * blocks + block
            for index, line in enumerate((gained[block : block + 1], squares[block : block + 1])):
                kept[index] = kept[index] + jnp.where(hit, line, 0.0)
    lane = lax.broadcasted_iota(jnp.int32, (REQ, size), 1)
    high = kept[1].astype(BF16).astype(F32)
    tail[...] = jnp.zeros_like(tail)
    tail[:REQ, :] = kept[0]
    tail[REQ : 2 * REQ, :] = jnp.where(lane == 0, high, jnp.where(lane == 1, kept[1] - high, 0.0))
    own = own_rows_ref.shape[0]
    for member in range(GROUP):
        out_ref[member, size : size + own, :] = own_rows_ref[...]
        out_ref[member, size + own :, :] = tail[...].astype(BF16)


def output_kernel(s_ref, qa_ref, own_ref, gate_ref, gain_ref, gated_ref):
    blocks, heads, block_len, dk = qa_ref.shape
    tok = blocks * block_len
    dv = own_ref.shape[3]
    for head in range(heads):
        state = jnp.concatenate([s_ref[2 * head], s_ref[2 * head + 1]], axis=1)
        out = dot(qa_ref[:, head].reshape(tok, dk), state) + own_ref[:, head].reshape(tok, dv)
        span = slice(head * dv, (head + 1) * dv)
        gated_ref[:, span] = (rms_scale(out, gain_ref[...]) * gate_ref[:, span]).astype(BF16)


def mix_kernel(meta_ref, gated_ref, w_ref, x_ref, one_ref, two_ref, three_ref, here_ref):
    step = pl.program_id(0)
    value = dot(gated_ref[...], w_ref[...])
    for place, ref in enumerate((one_ref, two_ref, three_ref)):

        @pl.when(step == place)
        def _():
            ref[...] = value.astype(BF16)

    @pl.when(step == pl.num_programs(0) - 1)
    def _():
        here_ref[...] = value + x_ref[...].astype(F32)


def rows_kernel(meta_ref, s_hbm, w_hbm, send_ref, rows_ref, w_ref, sums, lines, sems):
    dk = rows_ref.shape[2]
    dv = 2 * dk
    heads = w_ref.shape[0] // dv
    share = w_ref.shape[1] // 4
    own = rows_ref.shape[1] - PAD
    first_copy = pltpu.make_async_copy(
        s_hbm.at[:, pl.ds(s_hbm.shape[1] - rows_ref.shape[1], rows_ref.shape[1]), :], rows_ref, sems.at[heads]
    )
    first_copy.start()
    copies = []
    for head in range(heads):
        span = pl.ds(head * dv, dv)
        copies.append(pltpu.make_async_copy(w_hbm.at[span, :], w_ref.at[span, :], sems.at[head]))
        copies[-1].start()
    first_copy.wait()
    total = rows_ref[0, :own].astype(F32)
    for member in range(1, GROUP):
        total = total + rows_ref[member, :own].astype(F32)
    lines[...] = total
    tails = [rows_ref[member, own:].astype(F32) for member in range(GROUP)]
    gated = []
    for head in range(heads):
        both = tails[2 * head][REQ : 2 * REQ] + tails[2 * head + 1][REQ : 2 * REQ]
        scale = lax.rsqrt(jnp.sum(both, axis=1, keepdims=True) / dv + EPS)
        halves = []
        for member in (2 * head, 2 * head + 1):
            halves.append(tails[member][:REQ] * scale * lines[member * REQ : (member + 1) * REQ, :])
        gated.append(jnp.concatenate(halves, axis=1).astype(BF16))
    mixed = None
    for head in range(heads):
        copies[head].wait()
        value = dot(gated[head], w_ref[head * dv : (head + 1) * dv, :])
        mixed = value if mixed is None else mixed + value
    sums[...] = mixed
    for place in range(share // dk):
        at = pl.multiple_of(meta_ref[REQ + 1] * share + place * dk, dk)
        first = (GROUP + place) * REQ
        sums[:, pl.ds(at, dk)] += lines[first : first + REQ, :]
    value = sums[...].astype(BF16)
    for target in range(send_ref.shape[0]):
        send_ref[target] = value


def head_kernel(lasts_ref, gain_ref, w_ref, out_ref):
    last = jnp.sum(lasts_ref[...].astype(F32), axis=0).astype(BF16).astype(F32)
    final = rms_scale(last, gain_ref[...]).astype(BF16)
    best = jnp.max(dot(final, w_ref[...]), axis=1, keepdims=True)
    place, lane = iotas(best.shape[0], out_ref.shape[2])
    row = jnp.sum(jnp.where(place == lane, best, 0.0), axis=0, keepdims=True)
    out_ref[...] = jnp.broadcast_to(row[None], out_ref.shape)


def states_kernel(a_ref, b_ref, s_ref, out_ref):
    heads = a_ref.shape[1]
    for head in range(heads):
        state = jnp.concatenate([s_ref[2 * head], s_ref[2 * head + 1]], axis=1)
        high, low = split(a_ref[0, head])
        out_ref[0, head] = dot(high, state) + dot(low, state) + b_ref[0, head]


REQ = 4


def body(
    states_in, lengths, attn_gain, w_query, w_key, w_value, w_gate, w_beta, w_alpha, decay_rate,
    decay_bias, conv_query, conv_key, conv_value, out_gain, w_out, final_gain, w_head,
):
    tok, model = states_in.shape
    heads = decay_rate.shape[0]
    dk = w_query.shape[1] // heads
    dv = w_value.shape[1] // heads
    blocks = tok // BLOCK_LEN
    seq_count = lax.axis_size("seq")
    tp_count = lax.axis_size("tp")
    piece = lax.axis_index("seq")
    shard = lax.axis_index("tp")
    share = model // tp_count
    rows_all = heads * BLOCK_LEN
    shape = jax.ShapeDtypeStruct
    params = lambda mib: pltpu.CompilerParams(vmem_limit_bytes=mib << 20)
    meta = jnp.concatenate([lengths, piece[None], shard[None]]).astype(jnp.int32)

    halo = lax.ppermute(states_in[tok - HALO :], "seq", [(i, i + 1) for i in range(seq_count - 1)])
    gain = attn_gain[None, :]
    maps, normed, qa, own, a_all, b_all = pl.pallas_call(
        maps_kernel,
        out_shape=(
            shape((2 * heads, 2 * dk + 2 * PAD, dk), BF16),
            pltpu.HBM((tok, model), BF16),
            pltpu.HBM((blocks, heads, BLOCK_LEN, dk), BF16),
            pltpu.HBM((blocks, heads, BLOCK_LEN, dv), F32),
            pltpu.HBM((blocks, heads, dk, dk), F32),
            pltpu.HBM((blocks, heads, dk, dv), F32),
        ),
        in_specs=[SMEM, VMEM] + [HBM] * 12,
        out_specs=(VMEM,) + (HBM,) * 5,
        scratch_shapes=[
            pltpu.VMEM((HALO + tok, model), BF16),
            pltpu.VMEM((HALO + tok, 2 * heads * dk + heads * dv), F32),
            pltpu.VMEM((blocks, rows_all, dk), F32),
            pltpu.VMEM((blocks, rows_all, dk), F32),
            pltpu.VMEM((blocks, rows_all, dv), F32),
            pltpu.VMEM((blocks, heads, BLOCK_LEN, dk), BF16),
            pltpu.VMEM((blocks, heads, BLOCK_LEN, dv), F32),
            pltpu.VMEM((blocks, heads, dk, dk), F32),
            pltpu.VMEM((blocks, heads, dk, dv), F32),
            pltpu.SemaphoreType.DMA((4, blocks)),
            pltpu.VMEM((tok, 128), F32),
            pltpu.VMEM((tok, model), BF16),
            pltpu.VMEM((1, model), F32),
            pltpu.VMEM((heads, model), BF16),
            pltpu.VMEM((heads, model), BF16),
            pltpu.VMEM((1, heads), F32),
            pltpu.VMEM((1, heads), F32),
            pltpu.VMEM(w_query.shape, BF16),
            pltpu.VMEM(w_key.shape, BF16),
            pltpu.VMEM(w_value.shape, BF16),
            pltpu.VMEM(conv_query.shape, F32),
            pltpu.VMEM(conv_key.shape, F32),
            pltpu.VMEM(conv_value.shape, F32),
            pltpu.SemaphoreType.DMA((12,)),
            pltpu.SemaphoreType.DMA((1,)),
        ],
        compiler_params=params(40),
        name="maps_kernel",
    )(
        meta,
        halo,
        *hbm(
            states_in, gain, w_beta.T, w_alpha.T, decay_rate[None, :], decay_bias[None, :], w_query, w_key, w_value,
            conv_query, conv_key, conv_value,
        ),
    )

    got = group_exchange(maps)
    gate, own_rows = pl.pallas_call(
        gate_kernel,
        out_shape=(shape((tok, heads * dv), F32), shape((REQ * 3 * heads, dk), BF16)),
        grid_spec=pltpu.PrefetchScalarGridSpec(
            num_scalar_prefetch=1,
            grid=(heads,),
            in_specs=[
                whole(tok, model),
                pl.BlockSpec((model // heads, heads * dv), lambda i, m: (i, 0)),
                pl.BlockSpec((tok, share), lambda i, m: (0, m[REQ + 1])),
            ],
            out_specs=(whole(tok, heads * dv), whole(REQ * 3 * heads, dk)),
            scratch_shapes=[pltpu.VMEM((REQ * 3 * heads, dk), F32)],
        ),
        compiler_params=params(24),
        name="gate_kernel",
    )(meta, *hbm(normed, w_gate, states_in))
    got, gate, own_rows = lax.optimization_barrier((got, gate, own_rows))
    before, total = pl.pallas_call(
        scan_kernel,
        out_shape=(shape((GROUP, dk, 2 * dk), F32), shape((1, 2 * dk + PAD, dk), BF16)),
        in_specs=[VMEM],
        out_specs=(VMEM,) * 2,
        compiler_params=params(16),
        name="scan_kernel",
    )(got)
    one_back = shift_groups(total, 1)
    two_back = shift_groups(total[0, dk + PAD :], 2)
    rows_len = own_rows.shape[0] + PAD
    incoming = pl.pallas_call(
        apply_kernel,
        out_shape=shape((GROUP, dk + rows_len, dk), BF16),
        in_specs=[SMEM] + [VMEM] * 6,
        out_specs=VMEM,
        scratch_shapes=[pltpu.VMEM((PAD, dk), F32)],
        compiler_params=params(16),
        name="apply_kernel",
    )(meta, one_back, two_back, before, got, out_gain[None, :], own_rows)
    s_in = group_exchange(incoming)

    groups = seq_count // GROUP
    joint = [
        [(GROUP * group + member) * tp_count + column for group in range(groups) for column in range(tp_count)]
        for member in range(GROUP)
    ]
    sends = pl.pallas_call(
        rows_kernel,
        out_shape=shape((groups * tp_count, REQ, model), BF16),
        in_specs=[SMEM, HBM, HBM],
        out_specs=VMEM,
        scratch_shapes=[
            pltpu.VMEM((GROUP, rows_len, dk), BF16),
            pltpu.VMEM(w_out.shape, BF16),
            pltpu.VMEM((REQ, model), F32),
            pltpu.VMEM((rows_len - PAD, dk), F32),
            pltpu.SemaphoreType.DMA((heads + 1,)),
        ],
        compiler_params=params(24),
        name="rows_kernel",
    )(meta, *hbm(s_in, w_out))
    sends, s_after = lax.optimization_barrier((sends, s_in))
    lasts = lax.all_to_all(sends, ("seq", "tp"), 0, 0, axis_index_groups=joint)
    gated = pl.pallas_call(
        output_kernel,
        out_shape=shape((tok, heads * dv), BF16),
        grid=(1,),
        in_specs=[
            whole(2 * heads, dk, dk),
            whole(blocks, heads, BLOCK_LEN, dk),
            whole(blocks, heads, BLOCK_LEN, dv),
            whole(tok, heads * dv),
            whole(1, dv),
        ],
        out_specs=whole(tok, heads * dv),
        compiler_params=params(24),
        name="output_kernel",
    )(s_after, qa, own, gate, out_gain[None, :])

    turn = lambda i, m: (m[REQ + 1] + i + 1) % tp_count
    one, two, three, here = pl.pallas_call(
        mix_kernel,
        out_shape=(shape((tok, share), BF16),) * 3 + (shape((tok, share), F32),),
        grid_spec=pltpu.PrefetchScalarGridSpec(
            num_scalar_prefetch=1,
            grid=(tp_count,),
            in_specs=[
                whole(tok, heads * dv),
                pl.BlockSpec((heads * dv, share), lambda i, m: (0, turn(i, m))),
                pl.BlockSpec((tok, share), lambda i, m: (0, m[REQ + 1])),
            ],
            out_specs=(whole(tok, share),) * 4,
        ),
        compiler_params=params(24),
        name="mix_kernel",
    )(meta, gated, *hbm(w_out, states_in))

    rings = [[(i, (i + offset) % tp_count) for i in range(tp_count)] for offset in range(1, tp_count)]
    spread = pl.pallas_call(
        head_kernel,
        out_shape=shape((seq_count * tp_count, 1, 128), F32),
        grid=(1,),
        in_specs=[whole(groups * tp_count, REQ, model), whole(1, model), whole(*w_head.shape)],
        out_specs=whole(seq_count * tp_count, 1, 128),
        compiler_params=params(24),
        name="head_kernel",
    )(lasts, final_gain[None, :], w_head)
    spread, s_late = lax.optimization_barrier((spread, s_after))
    bests = lax.all_to_all(spread, ("seq", "tp"), 0, 0)
    block_states = pl.pallas_call(
        states_kernel,
        out_shape=shape((blocks, heads, dk, dv), F32),
        grid=(blocks,),
        in_specs=[
            pl.BlockSpec((1, heads, dk, dk), lambda i: (i, 0, 0, 0)),
            pl.BlockSpec((1, heads, dk, dv), lambda i: (i, 0, 0, 0)),
            pl.BlockSpec((2 * heads, dk, dk), lambda i: (0, 0, 0)),
        ],
        out_specs=pl.BlockSpec((1, heads, dk, dv), lambda i: (i, 0, 0, 0)),
        compiler_params=params(16),
        name="states_kernel",
    )(*hbm(a_all, b_all, s_late))

    mixed = here
    for ring, value in zip(rings, (one, two, three)):
        mixed = mixed + lax.ppermute(value, "tp", ring).astype(F32)
    hidden = mixed.astype(BF16)
    max_logit = jnp.max(bests[:, 0, :REQ], axis=0)
    return (hidden, block_states, max_logit)


def solution(mesh):
    return jax.shard_map(
        body,
        mesh=mesh,
        in_specs=(
            P("seq", None), P(), P(), P(None, "tp"), P(None, "tp"), P(None, "tp"), P(None, "tp"),
            P(None, "tp"), P(None, "tp"), P("tp"), P("tp"), P(None, "tp"), P(None, "tp"), P(None, "tp"),
            P(), P("tp", None), P(), P(None, ("seq", "tp")),
        ),
        out_specs=(P("seq", "tp"), P("seq", "tp", None, None), P()),
        check_vma=False,
    )
```

```python
import jax
import jax.numpy as jnp
from jax import lax
from jax.experimental import pallas as pl
from jax.experimental.pallas import tpu as pltpu
from jax.sharding import PartitionSpec as P


CONV = 4
BLOCK_LEN = 64
GROUP = 8
HALO = 16
PAD = 16
EPS = 1e-06
HIGH = lax.Precision.HIGHEST
F32 = jnp.float32
BF16 = jnp.bfloat16

VMEM = pl.BlockSpec(memory_space=pltpu.VMEM)
HBM = pl.BlockSpec(memory_space=pltpu.HBM)
SMEM = pl.BlockSpec(memory_space=pltpu.SMEM)


def whole(*dims):
    return pl.BlockSpec(dims, lambda *_: (0,) * len(dims))


def hbm(*values):
    return [pltpu.with_memory_space_constraint(value, pltpu.HBM) for value in values]


def rms_scale(values, gain):
    return values * lax.rsqrt(jnp.mean(values * values, axis=-1, keepdims=True) + EPS) * gain


def shift_groups(value, steps):
    count = lax.axis_size("seq")
    gap = steps * GROUP
    return lax.ppermute(value, "seq", [(source, (source + gap) % count) for source in range(count)])


def group_exchange(value):
    count = lax.axis_size("seq")
    groups = [list(range(first, first + GROUP)) for first in range(0, count, GROUP)]
    return lax.all_to_all(value, "seq", 0, 0, axis_index_groups=groups)


def dot(a, b):
    return jnp.dot(a, b, preferred_element_type=F32)


def dot_nt(a, b):
    return lax.dot_general(a, b, (((1,), (1,)), ((), ())), preferred_element_type=F32)


def dot_tn(a, b):
    return lax.dot_general(a, b, (((0,), (0,)), ((), ())), preferred_element_type=F32)


def split(a):
    high = a.astype(BF16)
    return high, (a - high.astype(F32)).astype(BF16)


def dot3(a, b):
    a_high, a_low = split(a)
    b_high, b_low = split(b)
    return dot(a_high, b_high) + dot(a_high, b_low) + dot(a_low, b_high)


def iotas(rows, cols):
    return (
        lax.broadcasted_iota(jnp.int32, (rows, cols), 0),
        lax.broadcasted_iota(jnp.int32, (rows, cols), 1),
    )


def last_blocks(meta_ref):
    place = lax.broadcasted_iota(jnp.int32, (REQ, 1), 0)
    final = jnp.zeros((REQ, 1), jnp.int32)
    end = jnp.int32(0)
    for request in range(REQ):
        end = end + meta_ref[request]
        final = jnp.where(place == request, end - 1, final)
    return final


def fill_scalars(normed, wb_ref, wa_ref, rate_ref, bias_ref, scal_ref):
    tok = normed.shape[0]
    heads = wb_ref.shape[0]
    beta = jax.nn.sigmoid(dot_nt(normed, wb_ref[...]))
    raw = dot_nt(normed, wa_ref[...]) + bias_ref[...]
    soft = jnp.maximum(raw, 0.0) + jnp.log1p(jnp.exp(-jnp.abs(raw)))
    log_decay = -rate_ref[...] * soft
    rows, cols = iotas(tok, tok)
    same = rows // BLOCK_LEN == cols // BLOCK_LEN
    run = jnp.dot((same & (rows >= cols)).astype(F32), log_decay, precision=HIGH, preferred_element_type=F32)
    full = jnp.dot(same.astype(F32), log_decay, precision=HIGH, preferred_element_type=F32)
    for place, value in enumerate((beta, run, jnp.exp(run), jnp.exp(full - run), jnp.exp(full))):
        scal_ref[:, place * heads : (place + 1) * heads] = value


def gate_kernel(meta_ref, normed_ref, w_gate_ref, x_ref, gate_ref, own_rows_ref, rows):
    tok = normed_ref.shape[0]
    depth = w_gate_ref.shape[0]
    lanes = own_rows_ref.shape[1]
    step = pl.program_id(0)

    @pl.when(step == 0)
    def _():
        gate_ref[...] = jnp.zeros_like(gate_ref)

    at = pl.multiple_of(step * depth, depth)
    gate_ref[...] += dot(normed_ref[:, pl.ds(at, depth)], w_gate_ref[...])

    @pl.when(step == pl.num_programs(0) - 1)
    def _():
        gate_ref[...] = jax.nn.silu(gate_ref[...])
        blocks = tok // BLOCK_LEN
        final = last_blocks(meta_ref)
        first = 0
        for ref in (gate_ref, x_ref):
            total = jnp.zeros((REQ, ref.shape[1]), F32)
            for block in range(blocks):
                end = (block + 1) * BLOCK_LEN
                line = ref[end - 8 : end, :].astype(F32)[7:8] if ref is gate_ref else ref[end - 16 : end, :].astype(F32)[15:16]
                total = total + jnp.where(final == meta_ref[REQ] * blocks + block, line, 0.0)
            for part in range(ref.shape[1] // lanes):
                rows[first : first + REQ, :] = total[:, part * lanes : (part + 1) * lanes]
                first += REQ
        own_rows_ref[...] = rows[...].astype(BF16)


def unit_lower_inverse(packed, spread, rows, cols):
    eye = (rows == cols).astype(F32)
    each = lambda fn, *lists: [fn(*items) for items in zip(*lists)]
    within = each(lambda m: jnp.where(rows // 8 == cols // 8, m, 0.0), packed)
    second = each(lambda m: dot3(m, spread(m)), within)
    fourth = each(lambda m: dot3(m, spread(m)), second)
    inverse = each(lambda m, n: dot3(eye - m, spread(eye + n)), within, second)
    inverse = each(lambda m, n: dot3(m, spread(eye + n)), inverse, fourth)
    width = 8
    while width < BLOCK_LEN:
        part = (rows // (2 * width) == cols // (2 * width)) & (rows // width != cols // width)
        left = each(lambda m, n: dot3(m, spread(jnp.where(part, n, 0.0))), inverse, packed)
        inverse = each(lambda m, n: m - dot3(n, spread(m)), inverse, left)
        width *= 2
    return inverse


def store_map(ref, at, a, b, eye):
    size = a.shape[0]
    diag = jnp.sum(jnp.where(eye, a, 0.0), axis=0, keepdims=True)
    high = diag.astype(BF16).astype(F32)
    low = diag - high
    place = lax.broadcasted_iota(jnp.int32, (PAD, size), 0)
    ref[at, :size, :] = jnp.where(eye, 0.0, a).astype(BF16)
    ref[at, size : size + PAD, :] = jnp.where(place == 0, high, jnp.where(place == 1, low, 0.0)).astype(BF16)
    ref[at, size + PAD : 2 * size + PAD, :] = b.astype(BF16)


def load_map(value, eye):
    size = value.shape[1]
    diag = value[size : size + PAD].astype(F32)
    a = value[:size].astype(F32) + jnp.where(eye, diag[0:1] + diag[1:2], 0.0)
    return a, value[size + PAD : 2 * size + PAD].astype(F32)


def maps_kernel(
    meta_ref, halo_ref, x_hbm, gain_hbm, wb_hbm, wa_hbm, rate_hbm, bias_hbm, wq_hbm, wk_hbm, wv_hbm,
    tq_hbm, tk_hbm, tv_hbm,
    maps_ref, normed_out, qa_out, own_out, a_ref, b_ref, lhs, pre, qs, ks, vs, qa_ref, own_ref, a_buf, b_buf, sems,
    scal_ref, x_ref, gain_ref, wb_ref, wa_ref, rate_ref, bias_ref, wq_ref, wk_ref, wv_ref,
    tq_ref, tk_ref, tv_ref, load_sems, normed_sem,
):
    loads = []
    for source, target in (
        (x_hbm, x_ref), (gain_hbm, gain_ref), (wq_hbm, wq_ref), (wk_hbm, wk_ref), (wb_hbm, wb_ref),
        (wa_hbm, wa_ref), (rate_hbm, rate_ref), (bias_hbm, bias_ref), (tq_hbm, tq_ref), (tk_hbm, tk_ref),
        (wv_hbm, wv_ref), (tv_hbm, tv_ref),
    ):
        loads.append(pltpu.make_async_copy(source, target, load_sems.at[len(loads)]))
        loads[-1].start()
    copies = []
    tok = x_ref.shape[0]
    blocks = tok // BLOCK_LEN
    heads = qa_ref.shape[1]
    dk = qa_ref.shape[3]
    dv = own_ref.shape[3]
    rows_all = heads * BLOCK_LEN
    keep = []
    first_block = meta_ref[REQ] * blocks
    for block in range(blocks):
        offset = jnp.int32(0)
        flag = jnp.float32(1.0)
        for request in range(REQ):
            flag = jnp.where(offset == first_block + block, 0.0, flag)
            offset = offset + meta_ref[request]
        keep.append(flag)
    loads[0].wait()
    loads[1].wait()
    lhs[:HALO, :] = rms_scale(halo_ref[...].astype(F32), gain_ref[...]).astype(BF16)
    lhs[HALO:, :] = rms_scale(x_ref[...].astype(F32), gain_ref[...]).astype(BF16)
    copies.append(pltpu.make_async_copy(lhs.at[pl.ds(HALO, tok), :], normed_out, normed_sem.at[0]))
    copies[-1].start()
    qk = heads * dk
    loads[2].wait()
    pre[:, :qk] = dot(lhs[...], wq_ref[...]).astype(BF16).astype(F32)
    for load in loads[3:10]:
        load.wait()
    pre[:, qk : 2 * qk] = dot(lhs[...], wk_ref[...]).astype(BF16).astype(F32)
    fill_scalars(lhs[HALO:, :], wb_ref, wa_ref, rate_ref, bias_ref, scal_ref)
    token = lax.broadcasted_iota(jnp.int32, (tok, 1), 0)
    masks = {}
    for lag in range(1, CONV):
        mask = jnp.ones((tok, 1), F32)
        for block in range(blocks):
            start = block * BLOCK_LEN
            mask = jnp.where((token >= start) & (token < start + lag), keep[block], mask)
        masks[lag] = mask

    def conv(first, taps_ref, at):
        total = None
        for tap in range(CONV):
            lag = CONV - 1 - tap
            part = pre[HALO - lag : HALO - lag + tok, first : first + dk] * taps_ref[tap : tap + 1, at : at + dk]
            if lag:
                part = part * masks[lag]
            total = part if total is None else total + part
        return jax.nn.silu(total)

    for head in range(heads):
        low = head * BLOCK_LEN
        for ref, base, taps_ref, scale in ((qs, 0, tq_ref, dk ** (-0.5)), (ks, qk, tk_ref, 1.0)):
            value = conv(base + head * dk, taps_ref, head * dk)
            value = value * (lax.rsqrt(jnp.sum(value * value, axis=-1, keepdims=True) + EPS) * scale)
            for block in range(blocks):
                ref[block, low : low + BLOCK_LEN, :] = value[block * BLOCK_LEN : (block + 1) * BLOCK_LEN]
    for load in loads[10:]:
        load.wait()
    pre[:, 2 * qk :] = dot(lhs[...], wv_ref[...]).astype(BF16).astype(F32)
    for head in range(heads):
        low = head * BLOCK_LEN
        for part in range(dv // dk):
            at = head * dv + part * dk
            value = conv(2 * qk + at, tv_ref, at)
            for block in range(blocks):
                vs[block, low : low + BLOCK_LEN, part * dk : (part + 1) * dk] = value[
                    block * BLOCK_LEN : (block + 1) * BLOCK_LEN
                ]

    rows, cols = iotas(rows_all, rows_all)
    same = rows // BLOCK_LEN == cols // BLOCK_LEN
    p_rows, p_cols = iotas(BLOCK_LEN, rows_all)
    p_cols = p_cols % BLOCK_LEN
    spread = lambda value: jnp.where(same, jnp.concatenate([value] * heads, axis=0), 0.0)
    k_rows, k_cols = iotas(dk, dk)
    eye = k_rows == k_cols

    def column(place, block):
        span = slice(block * BLOCK_LEN, (block + 1) * BLOCK_LEN)
        at = place * heads
        return jnp.concatenate([scal_ref[span, at + head : at + head + 1] for head in range(heads)], axis=0)

    betas = [column(0, block) for block in range(blocks)]
    growths = [column(2, block) for block in range(blocks)]
    kbs = [ks[block].astype(BF16) for block in range(blocks)]
    p_head = lax.broadcasted_iota(jnp.int32, (BLOCK_LEN, rows_all), 1) // BLOCK_LEN
    p_lower = p_rows >= p_cols
    p_strict = p_rows > p_cols

    def choose(items):
        value = items[0]
        for head in range(1, heads):
            value = jnp.where(p_head == head, items[head], value)
        return value

    def pack(full):
        return choose([full[head * BLOCK_LEN : (head + 1) * BLOCK_LEN] for head in range(heads)])

    def beside(place, block):
        span = slice(block * BLOCK_LEN, (block + 1) * BLOCK_LEN)
        return choose([scal_ref[span, place * heads + head : place * heads + head + 1] for head in range(heads)])

    packed, scores = [], []
    for block in range(blocks):
        run = beside(1, block)
        across = jnp.sum(jnp.where(p_rows == p_cols, run, 0.0), axis=0, keepdims=True)
        decay = jnp.where(p_lower, jnp.exp(jnp.where(p_lower, run - across, 0.0)), 0.0)
        gram = pack(dot_nt(kbs[block], kbs[block]))
        packed.append(jnp.where(p_strict, beside(0, block) * gram * decay, 0.0))
        scores.append(spread(pack(dot_nt(qs[block].astype(BF16), kbs[block])) * decay).astype(BF16))
    inverses = unit_lower_inverse(packed, spread, p_rows, p_cols)
    wus = []
    for block in range(blocks):
        right = jnp.concatenate([(betas[block] * growths[block]) * ks[block], betas[block] * vs[block]], axis=1)
        wus.append(dot(spread(inverses[block]).astype(BF16), right.astype(BF16)).astype(BF16))
    q_effs, owns, tails = [], [], []
    for block in range(blocks):
        mixed = dot(scores[block], wus[block])
        q_effs.append((growths[block] * qs[block] - mixed[:, :dk]).astype(BF16))
        owns.append(mixed[:, dk:])
        tails.append((column(3, block) * ks[block]).astype(BF16))

    spans = [slice(head * BLOCK_LEN, (head + 1) * BLOCK_LEN) for head in range(heads)]
    joints = [None] * heads
    tail_place = lax.broadcasted_iota(jnp.int32, (PAD, dk), 0)
    for block in range(blocks):
        for head, span in enumerate(spans):
            grown = dot_tn(tails[block][span], wus[block][span])
            at = 4 * heads + head
            last = scal_ref[block * BLOCK_LEN : block * BLOCK_LEN + 1, at : at + 1]
            shrink, add = grown[:, :dk], grown[:, dk:]
            if block == 0:
                qa_ref[block, head] = (q_effs[block][span].astype(F32) * keep[0]).astype(BF16)
                own_ref[block, head] = owns[block][span]
                a_run = (jnp.where(eye, last, 0.0) - shrink) * keep[0]
                b_run = add
            else:
                joint = joints[head] * keep[block]
                joint_b = joint.astype(BF16)
                seen = dot(q_effs[block][span], joint_b)
                qa_ref[block, head] = seen[:, :dk].astype(BF16)
                own_ref[block, head] = seen[:, dk:] + owns[block][span]
                joint = last * joint - dot(shrink.astype(BF16), joint_b)
                a_run = joint[:, :dk]
                b_run = joint[:, dk:] + add
            joints[head] = jnp.concatenate([a_run, b_run], axis=1)
            a_buf[block, head] = a_run
            b_buf[block, head] = b_run
            if block == blocks - 1:
                for part in range(2):
                    to = 2 * head + part
                    store_map(maps_ref, to, a_run, b_run[:, part * dk : (part + 1) * dk], eye)
                    lines = []
                    for row in range(blocks):
                        lines.append(qa_ref[row, head, BLOCK_LEN - 1 :, :].astype(F32))
                    for row in range(blocks):
                        lines.append(own_ref[row, head, BLOCK_LEN - 1 :, part * dk : (part + 1) * dk])
                    tail_rows = jnp.zeros((PAD, dk), F32)
                    for row, line in enumerate(lines):
                        tail_rows = jnp.where(tail_place == row, line, tail_rows)
                    maps_ref[to, 2 * dk + PAD :, :] = tail_rows.astype(BF16)
        for place, (buf, ref) in enumerate(
            ((qa_ref, qa_out), (own_ref, own_out), (a_buf, a_ref), (b_buf, b_ref))
        ):
            copies.append(pltpu.make_async_copy(buf.at[block], ref.at[block], sems.at[place, block]))
            copies[-1].start()
    for copy in copies:
        copy.wait()


def scan_kernel(got_ref, before_ref, total_ref):
    size = got_ref.shape[2]
    rows, cols = iotas(size, size)
    eye = rows == cols
    run = None
    for member in range(GROUP):
        a, b = load_map(got_ref[member], eye)
        if run is None:
            before_ref[member] = jnp.concatenate([eye.astype(F32), jnp.zeros((size, size), F32)], axis=1)
            run = jnp.concatenate([a, b], axis=1)
        else:
            before_ref[member] = run
            run = dot3(a, run)
            run = jnp.concatenate([run[:, :size], run[:, size:] + b], axis=1)
    store_map(total_ref, 0, run[:, :size], run[:, size:], eye)


def apply_kernel(meta_ref, one_ref, two_ref, before_ref, got_ref, gain_ref, own_rows_ref, out_ref, tail):
    size = one_ref.shape[2]
    blocks = PAD // 4
    rows, cols = iotas(size, size)
    eye = rows == cols
    a, b = load_map(one_ref[0], eye)
    a_high, a_low = split(a)
    part = meta_ref[REQ] % 2
    group = meta_ref[REQ] // GROUP
    entering = jnp.where(group >= 2, dot(a_high, two_ref[...]) + dot(a_low, two_ref[...]), 0.0) + b
    e_high, e_low = split(jnp.where(group >= 1, entering, 0.0))
    gain = jnp.where(part == 0, gain_ref[:, :size], gain_ref[:, size:])
    final = last_blocks(meta_ref)
    kept = [jnp.zeros((REQ, size), F32), jnp.zeros((REQ, 1), F32)]
    for member in range(GROUP):
        p_high, p_low = split(before_ref[member, :, :size])
        value = dot(p_high, e_high) + dot(p_high, e_low) + dot(p_low, e_high) + before_ref[member, :, size:]
        state = value.astype(BF16)
        out_ref[member, :size, :] = state
        extra = got_ref[member, 2 * size + PAD :, :]
        out = dot(extra, state)[:blocks] + extra.astype(F32)[blocks : 2 * blocks]
        squares = jnp.sum(out * out, axis=1, keepdims=True)
        gained = out * gain
        for block in range(blocks):
            hit = final == (group * GROUP + member) * blocks + block
            for index, line in enumerate((gained[block : block + 1], squares[block : block + 1])):
                kept[index] = kept[index] + jnp.where(hit, line, 0.0)
    lane = lax.broadcasted_iota(jnp.int32, (REQ, size), 1)
    high = kept[1].astype(BF16).astype(F32)
    tail[...] = jnp.zeros_like(tail)
    tail[:REQ, :] = kept[0]
    tail[REQ : 2 * REQ, :] = jnp.where(lane == 0, high, jnp.where(lane == 1, kept[1] - high, 0.0))
    own = own_rows_ref.shape[0]
    for member in range(GROUP):
        out_ref[member, size : size + own, :] = own_rows_ref[...]
        out_ref[member, size + own :, :] = tail[...].astype(BF16)


def output_kernel(s_ref, qa_ref, own_ref, gate_ref, gain_ref, gated_ref):
    blocks, heads, block_len, dk = qa_ref.shape
    tok = blocks * block_len
    dv = own_ref.shape[3]
    for head in range(heads):
        state = jnp.concatenate([s_ref[2 * head], s_ref[2 * head + 1]], axis=1)
        out = dot(qa_ref[:, head].reshape(tok, dk), state) + own_ref[:, head].reshape(tok, dv)
        span = slice(head * dv, (head + 1) * dv)
        gated_ref[:, span] = (rms_scale(out, gain_ref[...]) * gate_ref[:, span]).astype(BF16)


def mix_kernel(meta_ref, gated_ref, w_ref, x_ref, one_ref, two_ref, three_ref, here_ref):
    step = pl.program_id(0)
    value = dot(gated_ref[...], w_ref[...])
    for place, ref in enumerate((one_ref, two_ref, three_ref)):

        @pl.when(step == place)
        def _():
            ref[...] = value.astype(BF16)

    @pl.when(step == pl.num_programs(0) - 1)
    def _():
        here_ref[...] = value + x_ref[...].astype(F32)


def rows_kernel(meta_ref, s_hbm, w_hbm, send_ref, rows_ref, w_ref, sums, lines, sems):
    dk = rows_ref.shape[2]
    dv = 2 * dk
    heads = w_ref.shape[0] // dv
    share = w_ref.shape[1] // 4
    own = rows_ref.shape[1] - PAD
    first_copy = pltpu.make_async_copy(
        s_hbm.at[:, pl.ds(s_hbm.shape[1] - rows_ref.shape[1], rows_ref.shape[1]), :], rows_ref, sems.at[heads]
    )
    first_copy.start()
    copies = []
    for head in range(heads):
        span = pl.ds(head * dv, dv)
        copies.append(pltpu.make_async_copy(w_hbm.at[span, :], w_ref.at[span, :], sems.at[head]))
        copies[-1].start()
    first_copy.wait()
    total = rows_ref[0, :own].astype(F32)
    for member in range(1, GROUP):
        total = total + rows_ref[member, :own].astype(F32)
    lines[...] = total
    tails = [rows_ref[member, own:].astype(F32) for member in range(GROUP)]
    gated = []
    for head in range(heads):
        both = tails[2 * head][REQ : 2 * REQ] + tails[2 * head + 1][REQ : 2 * REQ]
        scale = lax.rsqrt(jnp.sum(both, axis=1, keepdims=True) / dv + EPS)
        halves = []
        for member in (2 * head, 2 * head + 1):
            halves.append(tails[member][:REQ] * scale * lines[member * REQ : (member + 1) * REQ, :])
        gated.append(jnp.concatenate(halves, axis=1).astype(BF16))
    mixed = None
    for head in range(heads):
        copies[head].wait()
        value = dot(gated[head], w_ref[head * dv : (head + 1) * dv, :])
        mixed = value if mixed is None else mixed + value
    sums[...] = mixed
    for place in range(share // dk):
        at = pl.multiple_of(meta_ref[REQ + 1] * share + place * dk, dk)
        first = (GROUP + place) * REQ
        sums[:, pl.ds(at, dk)] += lines[first : first + REQ, :]
    value = sums[...].astype(BF16)
    for target in range(send_ref.shape[0]):
        send_ref[target] = value


def head_kernel(lasts_ref, gain_ref, w_ref, out_ref):
    last = jnp.sum(lasts_ref[...].astype(F32), axis=0).astype(BF16).astype(F32)
    final = rms_scale(last, gain_ref[...]).astype(BF16)
    best = jnp.max(dot(final, w_ref[...]), axis=1, keepdims=True)
    place, lane = iotas(best.shape[0], out_ref.shape[2])
    row = jnp.sum(jnp.where(place == lane, best, 0.0), axis=0, keepdims=True)
    out_ref[...] = jnp.broadcast_to(row[None], out_ref.shape)


def states_kernel(a_ref, b_ref, s_ref, out_ref):
    heads = a_ref.shape[1]
    for head in range(heads):
        state = jnp.concatenate([s_ref[2 * head], s_ref[2 * head + 1]], axis=1)
        high, low = split(a_ref[0, head])
        out_ref[0, head] = dot(high, state) + dot(low, state) + b_ref[0, head]


REQ = 4


def body(
    states_in, lengths, attn_gain, w_query, w_key, w_value, w_gate, w_beta, w_alpha, decay_rate,
    decay_bias, conv_query, conv_key, conv_value, out_gain, w_out, final_gain, w_head,
):
    tok, model = states_in.shape
    heads = decay_rate.shape[0]
    dk = w_query.shape[1] // heads
    dv = w_value.shape[1] // heads
    blocks = tok // BLOCK_LEN
    seq_count = lax.axis_size("seq")
    tp_count = lax.axis_size("tp")
    piece = lax.axis_index("seq")
    shard = lax.axis_index("tp")
    share = model // tp_count
    rows_all = heads * BLOCK_LEN
    shape = jax.ShapeDtypeStruct
    params = lambda mib: pltpu.CompilerParams(vmem_limit_bytes=mib << 20)
    meta = jnp.concatenate([lengths, piece[None], shard[None]]).astype(jnp.int32)

    halo = lax.ppermute(states_in[tok - HALO :], "seq", [(i, (i + 1) % seq_count) for i in range(seq_count)])
    gain = attn_gain[None, :]
    maps, normed, qa, own, a_all, b_all = pl.pallas_call(
        maps_kernel,
        out_shape=(
            shape((2 * heads, 2 * dk + 2 * PAD, dk), BF16),
            pltpu.HBM((tok, model), BF16),
            pltpu.HBM((blocks, heads, BLOCK_LEN, dk), BF16),
            pltpu.HBM((blocks, heads, BLOCK_LEN, dv), F32),
            pltpu.HBM((blocks, heads, dk, dk), F32),
            pltpu.HBM((blocks, heads, dk, dv), F32),
        ),
        in_specs=[SMEM, VMEM] + [HBM] * 12,
        out_specs=(VMEM,) + (HBM,) * 5,
        scratch_shapes=[
            pltpu.VMEM((HALO + tok, model), BF16),
            pltpu.VMEM((HALO + tok, 2 * heads * dk + heads * dv), F32),
            pltpu.VMEM((blocks, rows_all, dk), F32),
            pltpu.VMEM((blocks, rows_all, dk), F32),
            pltpu.VMEM((blocks, rows_all, dv), F32),
            pltpu.VMEM((blocks, heads, BLOCK_LEN, dk), BF16),
            pltpu.VMEM((blocks, heads, BLOCK_LEN, dv), F32),
            pltpu.VMEM((blocks, heads, dk, dk), F32),
            pltpu.VMEM((blocks, heads, dk, dv), F32),
            pltpu.SemaphoreType.DMA((4, blocks)),
            pltpu.VMEM((tok, 128), F32),
            pltpu.VMEM((tok, model), BF16),
            pltpu.VMEM((1, model), F32),
            pltpu.VMEM((heads, model), BF16),
            pltpu.VMEM((heads, model), BF16),
            pltpu.VMEM((1, heads), F32),
            pltpu.VMEM((1, heads), F32),
            pltpu.VMEM(w_query.shape, BF16),
            pltpu.VMEM(w_key.shape, BF16),
            pltpu.VMEM(w_value.shape, BF16),
            pltpu.VMEM(conv_query.shape, F32),
            pltpu.VMEM(conv_key.shape, F32),
            pltpu.VMEM(conv_value.shape, F32),
            pltpu.SemaphoreType.DMA((12,)),
            pltpu.SemaphoreType.DMA((1,)),
        ],
        compiler_params=params(40),
        name="maps_kernel",
    )(
        meta,
        halo,
        *hbm(
            states_in, gain, w_beta.T, w_alpha.T, decay_rate[None, :], decay_bias[None, :], w_query, w_key, w_value,
            conv_query, conv_key, conv_value,
        ),
    )

    got = group_exchange(maps)
    gate, own_rows = pl.pallas_call(
        gate_kernel,
        out_shape=(shape((tok, heads * dv), F32), shape((REQ * 3 * heads, dk), BF16)),
        grid_spec=pltpu.PrefetchScalarGridSpec(
            num_scalar_prefetch=1,
            grid=(heads,),
            in_specs=[
                whole(tok, model),
                pl.BlockSpec((model // heads, heads * dv), lambda i, m: (i, 0)),
                pl.BlockSpec((tok, share), lambda i, m: (0, m[REQ + 1])),
            ],
            out_specs=(whole(tok, heads * dv), whole(REQ * 3 * heads, dk)),
            scratch_shapes=[pltpu.VMEM((REQ * 3 * heads, dk), F32)],
        ),
        compiler_params=params(24),
        name="gate_kernel",
    )(meta, *hbm(normed, w_gate, states_in))
    got, gate, own_rows = lax.optimization_barrier((got, gate, own_rows))
    before, total = pl.pallas_call(
        scan_kernel,
        out_shape=(shape((GROUP, dk, 2 * dk), F32), shape((1, 2 * dk + PAD, dk), BF16)),
        in_specs=[VMEM],
        out_specs=(VMEM,) * 2,
        compiler_params=params(16),
        name="scan_kernel",
    )(got)
    one_back = shift_groups(total, 1)
    two_back = shift_groups(total[0, dk + PAD :], 2)
    rows_len = own_rows.shape[0] + PAD
    incoming = pl.pallas_call(
        apply_kernel,
        out_shape=shape((GROUP, dk + rows_len, dk), BF16),
        in_specs=[SMEM] + [VMEM] * 6,
        out_specs=VMEM,
        scratch_shapes=[pltpu.VMEM((PAD, dk), F32)],
        compiler_params=params(16),
        name="apply_kernel",
    )(meta, one_back, two_back, before, got, out_gain[None, :], own_rows)
    s_in = group_exchange(incoming)

    groups = seq_count // GROUP
    joint = [
        [(GROUP * group + member) * tp_count + column for group in range(groups) for column in range(tp_count)]
        for member in range(GROUP)
    ]
    sends = pl.pallas_call(
        rows_kernel,
        out_shape=shape((groups * tp_count, REQ, model), BF16),
        in_specs=[SMEM, HBM, HBM],
        out_specs=VMEM,
        scratch_shapes=[
            pltpu.VMEM((GROUP, rows_len, dk), BF16),
            pltpu.VMEM(w_out.shape, BF16),
            pltpu.VMEM((REQ, model), F32),
            pltpu.VMEM((rows_len - PAD, dk), F32),
            pltpu.SemaphoreType.DMA((heads + 1,)),
        ],
        compiler_params=params(24),
        name="rows_kernel",
    )(meta, *hbm(s_in, w_out))
    sends, s_after = lax.optimization_barrier((sends, s_in))
    lasts = lax.all_to_all(sends, ("seq", "tp"), 0, 0, axis_index_groups=joint)
    gated = pl.pallas_call(
        output_kernel,
        out_shape=shape((tok, heads * dv), BF16),
        grid=(1,),
        in_specs=[
            whole(2 * heads, dk, dk),
            whole(blocks, heads, BLOCK_LEN, dk),
            whole(blocks, heads, BLOCK_LEN, dv),
            whole(tok, heads * dv),
            whole(1, dv),
        ],
        out_specs=whole(tok, heads * dv),
        compiler_params=params(24),
        name="output_kernel",
    )(s_after, qa, own, gate, out_gain[None, :])

    turn = lambda i, m: (m[REQ + 1] + i + 1) % tp_count
    one, two, three, here = pl.pallas_call(
        mix_kernel,
        out_shape=(shape((tok, share), BF16),) * 3 + (shape((tok, share), F32),),
        grid_spec=pltpu.PrefetchScalarGridSpec(
            num_scalar_prefetch=1,
            grid=(tp_count,),
            in_specs=[
                whole(tok, heads * dv),
                pl.BlockSpec((heads * dv, share), lambda i, m: (0, turn(i, m))),
                pl.BlockSpec((tok, share), lambda i, m: (0, m[REQ + 1])),
            ],
            out_specs=(whole(tok, share),) * 4,
        ),
        compiler_params=params(24),
        name="mix_kernel",
    )(meta, gated, *hbm(w_out, states_in))

    rings = [[(i, (i + offset) % tp_count) for i in range(tp_count)] for offset in range(1, tp_count)]
    spread = pl.pallas_call(
        head_kernel,
        out_shape=shape((seq_count * tp_count, 1, 128), F32),
        grid=(1,),
        in_specs=[whole(groups * tp_count, REQ, model), whole(1, model), whole(*w_head.shape)],
        out_specs=whole(seq_count * tp_count, 1, 128),
        compiler_params=params(24),
        name="head_kernel",
    )(lasts, final_gain[None, :], w_head)
    spread, s_late = lax.optimization_barrier((spread, s_after))
    bests = lax.all_to_all(spread, ("seq", "tp"), 0, 0)
    block_states = pl.pallas_call(
        states_kernel,
        out_shape=shape((blocks, heads, dk, dv), F32),
        grid=(blocks,),
        in_specs=[
            pl.BlockSpec((1, heads, dk, dk), lambda i: (i, 0, 0, 0)),
            pl.BlockSpec((1, heads, dk, dv), lambda i: (i, 0, 0, 0)),
            pl.BlockSpec((2 * heads, dk, dk), lambda i: (0, 0, 0)),
        ],
        out_specs=pl.BlockSpec((1, heads, dk, dv), lambda i: (i, 0, 0, 0)),
        compiler_params=params(16),
        name="states_kernel",
    )(*hbm(a_all, b_all, s_late))

    mixed = here
    for ring, value in zip(rings, (one, two, three)):
        mixed = mixed + lax.ppermute(value, "tp", ring).astype(F32)
    hidden = mixed.astype(BF16)
    max_logit = jnp.max(bests[:, 0, :REQ], axis=0)
    return (hidden, block_states, max_logit)


def solution(mesh):
    return jax.shard_map(
        body,
        mesh=mesh,
        in_specs=(
            P("seq", None), P(), P(), P(None, "tp"), P(None, "tp"), P(None, "tp"), P(None, "tp"),
            P(None, "tp"), P(None, "tp"), P("tp"), P("tp"), P(None, "tp"), P(None, "tp"), P(None, "tp"),
            P(), P("tp", None), P(), P(None, ("seq", "tp")),
        ),
        out_specs=(P("seq", "tp"), P("seq", "tp", None, None), P()),
        check_vma=False,
    )
```
